1024 devices in a mesh: row: 16 (over y, z_lo), col: 64 (over x, z_hi, core).
Axes of the slice: x: 8, y: 8, z: 8 (z_hi: 4, z_lo: 2; z = z_hi * 2 + z_lo), core: 2. Of those that a mesh axis runs over, the one named last changes fastest.
Arguments:
- fields: float32 [5, 1, 4096, 2048], P(None, None, 'col', 'row'), may hold values from -3 to 150, as said below
Outputs:
- updated: float32 [5, 1, 4096, 2048], P(None, None, 'col', 'row')
The draws below stay inside these ranges and needn't reach their ends.
Inputs may be any that keep to these rules, and one draw needn't show every extreme that they name: `fields`: field 0 is the density and field 4 the total energy; density and pressure are positive in every cell.
All inputs are finite; a program needn't handle non-finite values.
Results may differ from the reference program's by a relative error of at most 0.0003.
Values sent between devices are 32-bit elements; how exact they have to be, the bound alone decides.
No kernel may reach another device: no remote copies, remote signals or barrier semaphores. Data moves between devices by JAX's collectives and lax.ppermute only.
A program may use at most 32 MiB of HBM per device.

```python
import jax
import jax.numpy as jnp
from jax import lax

NX = 2048
SLAB = 1
NY = 4096


GAMMA = 1.4


BUBBLE_RADIUS = 12.0


def draw_fields(key, part):
    keys = jax.random.split(key, 9)
    shape_three = (SLAB, NY, NX)
    column_cell = jnp.arange(NX, dtype=jnp.float32)[None, None, :]
    row_cell = jnp.arange(NY, dtype=jnp.float32)[None, :, None]
    column_pos = column_cell / NX
    row_pos = row_cell / NY
    ramp = 1.0 + 4.0 * column_pos + 4.0 * row_pos
    centre_x = jax.random.uniform(keys[5], (), jnp.float32, 0.25, 0.75) * NX
    centre_y = jax.random.uniform(keys[6], (), jnp.float32, 0.1, 0.9) * NY
    heating = jax.random.uniform(keys[7], (), jnp.float32, 10.0, 16.0)
    dilution = jax.random.uniform(keys[8], (), jnp.float32, 2.0, 3.0)
    offset_x = column_cell - centre_x
    offset_y = row_cell - centre_y
    bubble = jnp.exp(-(offset_x * offset_x + offset_y * offset_y) / (BUBBLE_RADIUS * BUBBLE_RADIUS))
    density = jax.random.uniform(keys[0], shape_three, jnp.float32, 1.0, 2.0)
    velocity_x = jax.random.uniform(keys[1], shape_three, jnp.float32, -0.5, 0.5)
    velocity_y = jax.random.uniform(keys[2], shape_three, jnp.float32, -0.5, 0.5)
    velocity_z = jax.random.uniform(keys[3], shape_three, jnp.float32, -0.5, 0.5)
    base_pressure = jax.random.uniform(keys[4], shape_three, jnp.float32, 1.0, 2.0)
    density = density / (1.0 + dilution * bubble)
    pressure = base_pressure * (ramp + heating * bubble)
    speed_square = velocity_x * velocity_x + velocity_y * velocity_y + velocity_z * velocity_z
    energy = pressure / (GAMMA - 1.0) + 0.5 * density * speed_square
    return jnp.stack([density, density * velocity_x, density * velocity_y, density * velocity_z, energy])


def setup_inputs(seed: int = 0) -> dict:
    splits = jax.random.split(jax.random.key(seed), 2)
    return {
        "fields": draw_fields(jax.random.fold_in(splits[1], 71), 0),
    }


GAMMA = 1.4
COURANT = 0.3

def window_slice(profile, begin_at, trim_end, direction_axis):
    direction_axis = direction_axis % profile.ndim
    return lax.slice_in_dim(profile, begin_at, profile.shape[direction_axis] - trim_end, axis=direction_axis)

def minmod(first_slope, second_slope):
    return 0.5 * (jnp.sign(first_slope) + jnp.sign(second_slope)) * jnp.minimum(jnp.abs(first_slope), jnp.abs(second_slope))

def rebuild(profile, direction_axis):
    far_left = window_slice(profile, 0, 3, direction_axis)
    near_left = window_slice(profile, 1, 2, direction_axis)
    near_right = window_slice(profile, 2, 1, direction_axis)
    far_right = window_slice(profile, 3, 0, direction_axis)
    edge_value = 7.0 / 12.0 * (near_left + near_right) - 1.0 / 12.0 * (far_left + far_right)
    edge_value = jnp.clip(edge_value, jnp.minimum(near_left, near_right), jnp.maximum(near_left, near_right))
    centre = window_slice(profile, 2, 2, direction_axis)
    lower_edge = window_slice(edge_value, 0, 1, direction_axis)
    upper_edge = window_slice(edge_value, 1, 0, direction_axis)
    upper_jump = upper_edge - centre
    lower_jump = centre - lower_edge
    right_face = centre + minmod(upper_jump, 2.0 * lower_jump)
    left_face = centre - minmod(lower_jump, 2.0 * upper_jump)
    return (window_slice(right_face, 0, 1, direction_axis), window_slice(left_face, 1, 0, direction_axis))

def face_terms(density, velocity, pressure, normal):
    speed_square = velocity[0] * velocity[0] + velocity[1] * velocity[1] + velocity[2] * velocity[2]
    energy = pressure / (GAMMA - 1.0) + 0.5 * density * speed_square
    normal_speed = velocity[normal - 1]
    conserved = [density, density * velocity[0], density * velocity[1], density * velocity[2], energy]
    face_flux = [density * normal_speed]
    for component in range(3):
        momentum_flux = density * normal_speed * velocity[component]
        if component == normal - 1:
            momentum_flux = momentum_flux + pressure
        face_flux.append(momentum_flux)
    face_flux.append(normal_speed * (energy + pressure))
    signal = jnp.abs(normal_speed) + jnp.sqrt(GAMMA * pressure / density)
    return (conserved, face_flux, signal)

def primitives(cells):
    density = cells[0]
    velocity = [cells[1] / density, cells[2] / density, cells[3] / density]
    kinetic = 0.5 * density * (velocity[0] * velocity[0] + velocity[1] * velocity[1] + velocity[2] * velocity[2])
    pressure = (GAMMA - 1.0) * (cells[4] - kinetic)
    return (density, velocity, pressure)

def courant(cells):
    density, velocity, pressure = primitives(cells)
    return jnp.maximum(jnp.abs(velocity[0]), jnp.abs(velocity[1])) + jnp.sqrt(GAMMA * pressure / density)

def sweep_along(padded, time_step, direction_axis, normal):
    density, velocity, pressure = primitives(padded)
    face_pairs = [rebuild(profile, direction_axis) for profile in [density, velocity[0], velocity[1], velocity[2], pressure]]
    left_states = [pair[0] for pair in face_pairs]
    right_states = [pair[1] for pair in face_pairs]
    left_conserved, left_flux, left_signal = face_terms(left_states[0], left_states[1:4], left_states[4], normal)
    right_conserved, right_flux, right_signal = face_terms(right_states[0], right_states[1:4], right_states[4], normal)
    signal = jnp.maximum(left_signal, right_signal)
    results = []
    for component in range(5):
        face_flux = 0.5 * (left_flux[component] + right_flux[component]) - 0.5 * signal * (right_conserved[component] - left_conserved[component])
        difference = window_slice(face_flux, 1, 0, direction_axis) - window_slice(face_flux, 0, 1, direction_axis)
        results.append(window_slice(padded[component], 3, 3, direction_axis) - time_step * difference)
    return jnp.stack(results)

def reference(fields):
    planes = jnp.moveaxis(fields, 1, 0)
    peak_speed = jnp.max(lax.map(lambda slab_plane: jnp.max(courant(slab_plane)), planes))
    time_step = COURANT / peak_speed

    def advance(slab_plane):
        padded = jnp.concatenate([slab_plane[..., -3:], slab_plane, slab_plane[..., :3]], axis=-1)
        halfway = sweep_along(padded, time_step, -1, 1)
        padded = jnp.concatenate([halfway[..., -3:, :], halfway, halfway[..., :3, :]], axis=-2)
        return sweep_along(padded, time_step, -2, 2)
    result = lax.map(advance, planes)
    return jnp.moveaxis(result, 0, 1)
```

```python
import jax
import jax.numpy as jnp
from jax import lax
from jax.experimental import pallas as pl
from jax.experimental.pallas import tpu as pltpu
from jax.sharding import Mesh
from jax.sharding import PartitionSpec as P

ROW = ("row_0", "row_1")
COL = ("col_0", "col_1", "col_2")

GAMMA = 1.4
COURANT = 0.3
WIDTH = 3
FIELDS = 5
PACKED = 16
VMEM = pl.BlockSpec(memory_space=pltpu.VMEM)
SMEM = pl.BlockSpec(memory_space=pltpu.SMEM)


def minmod(first, second):
    low = jnp.minimum(first, second)
    high = jnp.maximum(first, second)
    return jnp.maximum(low, 0.0) + jnp.minimum(high, 0.0)


def shifted(profile, step, axis):
    return pltpu.roll(profile, (-step) % profile.shape[axis], axis)


def primitives(cells):
    inverse = 1.0 / cells[0]
    velocity = [cells[k] * inverse for k in (1, 2, 3)]
    kinetic = 0.5 * (cells[1] * velocity[0] + cells[2] * velocity[1] + cells[3] * velocity[2])
    return [cells[0], *velocity, (GAMMA - 1.0) * (cells[4] - kinetic)], inverse


def rebuild(profile, axis):
    after = shifted(profile, 1, axis)
    edge = 7.0 / 12.0 * (profile + after) - 1.0 / 12.0 * (
        shifted(profile, -1, axis) + shifted(profile, 2, axis)
    )
    edge = jnp.clip(edge, jnp.minimum(profile, after), jnp.maximum(profile, after))
    rise = edge - profile
    fall = profile - shifted(edge, -1, axis)
    right = profile + minmod(rise, 2.0 * fall)
    left = profile - minmod(fall, 2.0 * rise)
    return right, shifted(left, 1, axis)


def face_terms(state, normal):
    density, pressure = state[0], state[4]
    speed = state[normal]
    momentum = [density * state[k] for k in (1, 2, 3)]
    square = state[1] * momentum[0] + state[2] * momentum[1] + state[3] * momentum[2]
    energy = pressure * (1.0 / (GAMMA - 1.0)) + 0.5 * square
    conserved = [density, *momentum, energy]
    flux = [momentum[normal - 1]]
    for k in range(3):
        term = speed * momentum[k]
        flux.append(term + pressure if k == normal - 1 else term)
    flux.append(speed * (energy + pressure))
    return conserved, flux, jnp.abs(speed) + jnp.sqrt(GAMMA * pressure / density)


def flux_difference(cells, axis, normal):
    states, _ = primitives(cells)
    faces = [rebuild(profile, axis) for profile in states]
    left = face_terms([pair[0] for pair in faces], normal)
    right = face_terms([pair[1] for pair in faces], normal)
    signal = 0.5 * jnp.maximum(left[2], right[2])
    differences = []
    for k in range(FIELDS):
        flux = 0.5 * (left[1][k] + right[1][k]) - signal * (right[0][k] - left[0][k])
        differences.append(flux - shifted(flux, -1, axis))
    return differences


def start_kernel(fields_ref, peak_ref, first_ref, last_ref):
    rows = fields_ref.shape[1]
    for k in range(FIELDS):
        first_ref[k * WIDTH : (k + 1) * WIDTH, :] = fields_ref[k, :WIDTH, :]
        last_ref[k * WIDTH : (k + 1) * WIDTH, :] = fields_ref[k, rows - WIDTH :, :]
    first_ref[FIELDS * WIDTH :, :] = fields_ref[0, :1, :]
    last_ref[FIELDS * WIDTH :, :] = fields_ref[0, :1, :]
    (density, *velocity, pressure), _ = primitives([fields_ref[k] for k in range(FIELDS)])
    speed = jnp.maximum(jnp.abs(velocity[0]), jnp.abs(velocity[1]))
    speed = speed + jnp.sqrt(GAMMA * pressure / density)
    peak = jnp.max(speed, axis=0, keepdims=True)
    peak_ref[...] = jnp.broadcast_to(peak[None], peak_ref.shape)


def extended_rows(fields_ref, before_ref, after_ref, full_ref):
    rows = fields_ref.shape[1]
    for k in range(FIELDS):
        full_ref[k, :rows, :] = fields_ref[k]
        full_ref[k, rows : rows + 8, :] = fields_ref[k, :8, :]
        full_ref[k, rows : rows + WIDTH, :] = after_ref[k * WIDTH : (k + 1) * WIDTH, :]
        full_ref[k, rows + 8 - WIDTH : rows + 8, :] = before_ref[k * WIDTH : (k + 1) * WIDTH, :]


def side_kernel(me_ref, fields_ref, peaks_ref, before_ref, after_ref, send_ref, full_ref):
    count = send_ref.shape[0]
    rows, columns = fields_ref.shape[1:]
    extended_rows(fields_ref, before_ref, after_ref, full_ref)
    peak = jnp.max(peaks_ref[...], axis=0)
    lane = lax.broadcasted_iota(jnp.int32, (rows + 8, columns), 1)
    packed = jnp.zeros((rows + 8, columns), jnp.float32)
    for k in range(FIELDS):
        cells = full_ref[k]
        at = k * WIDTH
        ends = pltpu.roll(cells, (at + WIDTH) % columns, 1)
        starts = pltpu.roll(cells, PACKED + at, 1)
        packed = jnp.where((lane >= at) & (lane < at + WIDTH), ends, packed)
        packed = jnp.where((lane >= PACKED + at) & (lane < PACKED + at + WIDTH), starts, packed)
    pad = jnp.zeros((columns - rows - 8, columns), jnp.float32)
    turned = jnp.transpose(jnp.concatenate([packed, pad], axis=0))
    bottom = lax.broadcasted_iota(jnp.int32, (PACKED, columns), 0) == PACKED - 1
    ends = jnp.where(bottom, peak, turned[:PACKED])
    starts = jnp.where(bottom, peak, turned[PACKED : 2 * PACKED])
    for j in range(count):
        send_ref[j] = ends
    me = me_ref[0]
    send_ref[lax.rem(me + count - 1, count)] = starts


def sweep_kernel(me_ref, fields_ref, before_ref, after_ref, received_ref, out_ref, full_ref, half_ref):
    count = received_ref.shape[0]
    rows, columns = fields_ref.shape[1:]
    me = me_ref[0]
    peak = jnp.max(received_ref[...], axis=0)[PACKED - 1 :, :]
    time_step = COURANT / jnp.max(peak, axis=1, keepdims=True)
    extended_rows(fields_ref, before_ref, after_ref, full_ref)
    left = received_ref[lax.rem(me + count - 1, count)]
    right = received_ref[lax.rem(me + 1, count)]
    pad = jnp.zeros((columns - 2 * PACKED, columns), jnp.float32)
    turned = jnp.transpose(jnp.concatenate([right, left, pad], axis=0))
    step = jnp.broadcast_to(time_step, (8, columns))
    lane = lax.broadcasted_iota(jnp.int32, (8, columns), 1)
    for row in range(0, rows + 8, 8):
        strip = turned[row : row + 8]
        own = [full_ref[k, row : row + 8, :] for k in range(FIELDS)]
        cells = []
        for k in range(FIELDS):
            after = pltpu.roll(strip, (-k * WIDTH) % columns, 1)
            before = pltpu.roll(strip, (columns - WIDTH - PACKED - k * WIDTH) % columns, 1)
            side = jnp.where(lane < WIDTH, after, jnp.where(lane >= columns - WIDTH, before, own[k]))
            cells.append(jnp.concatenate([own[k], side], axis=1))
        change = flux_difference(cells, 1, 1)
        for k in range(FIELDS):
            half_ref[k, row : row + 8, :] = own[k] - step * change[k][:, :columns]
    cells = [half_ref[k] for k in range(FIELDS)]
    change = flux_difference(cells, 0, 2)
    for k in range(FIELDS):
        out_ref[k] = (cells[k] - time_step * change[k])[:rows]


def call(kernel, out_shape, n_smem, n_vmem, scratch=()):
    return pl.pallas_call(
        kernel,
        out_shape=out_shape,
        in_specs=[SMEM] * n_smem + [VMEM] * n_vmem,
        out_specs=jax.tree.map(lambda _: VMEM, out_shape),
        scratch_shapes=list(scratch),
    )


def f32(*shape):
    return jax.ShapeDtypeStruct(shape, jnp.float32)


def local(fields):
    rows, columns = fields.shape[2:]
    cells = fields.reshape(FIELDS, rows, columns)
    count_row, count_col = lax.axis_size(ROW), lax.axis_size(COL)
    me = lax.axis_index(ROW).astype(jnp.int32).reshape(1)
    full = pltpu.VMEM((FIELDS, rows + 8, columns), jnp.float32)
    packed = f32(PACKED, columns)

    peaks, first, last = call(start_kernel, (f32(count_col, 1, columns), packed, packed), 0, 1)(cells)
    up = [(i, (i + 1) % count_col) for i in range(count_col)]
    before = lax.ppermute(last, COL, up)
    after = lax.ppermute(first, COL, [(j, i) for i, j in up])
    peaks = lax.all_to_all(peaks, COL, 0, 0, tiled=True)
    send = call(side_kernel, f32(count_row, PACKED, columns), 1, 4, [full])(me, cells, peaks, before, after)
    received = lax.all_to_all(send, ROW, 0, 0, tiled=True)
    out = call(sweep_kernel, f32(FIELDS, rows, columns), 1, 4, [full, full])(
        me, cells, before, after, received
    )
    return out.reshape(fields.shape)


def solution(mesh):
    split = Mesh(mesh.devices.reshape(8, 2, 8, 4, 2), (*ROW, *COL))
    placed = (P(None, None, COL, ROW),)
    return jax.shard_map(
        local, mesh=split, in_specs=placed, out_specs=P(None, None, COL, ROW), check_vma=False
    )
```

```python
import jax
import jax.numpy as jnp
from jax import lax
from jax.experimental import pallas as pl
from jax.experimental.pallas import tpu as pltpu
from jax.sharding import Mesh
from jax.sharding import PartitionSpec as P

ROW = ("row_0", "row_1")
COL = ("col_0", "col_1", "col_2")

GAMMA = 1.4
COURANT = 0.3
WIDTH = 3
FIELDS = 5
PACKED = 16
VMEM = pl.BlockSpec(memory_space=pltpu.VMEM)
SMEM = pl.BlockSpec(memory_space=pltpu.SMEM)


def minmod(first, second):
    low = jnp.minimum(first, second)
    high = jnp.maximum(first, second)
    return jnp.maximum(low, 0.0) + jnp.minimum(high, 0.0)


def shifted(profile, step, axis):
    return pltpu.roll(profile, (-step) % profile.shape[axis], axis)


def primitives(cells):
    inverse = 1.0 / cells[0]
    velocity = [cells[k] * inverse for k in (1, 2, 3)]
    kinetic = 0.5 * (cells[1] * velocity[0] + cells[2] * velocity[1] + cells[3] * velocity[2])
    return [cells[0], *velocity, (GAMMA - 1.0) * (cells[4] - kinetic)], inverse


def rebuild(profile, axis):
    after = shifted(profile, 1, axis)
    edge = 7.0 / 12.0 * (profile + after) - 1.0 / 12.0 * (
        shifted(profile, -1, axis) + shifted(profile, 2, axis)
    )
    edge = jnp.clip(edge, jnp.minimum(profile, after), jnp.maximum(profile, after))
    rise = edge - profile
    fall = profile - shifted(edge, -1, axis)
    right = profile + minmod(rise, 2.0 * fall)
    left = profile - minmod(fall, 2.0 * rise)
    return right, shifted(left, 1, axis)


def face_terms(state, normal):
    density, pressure = state[0], state[4]
    speed = state[normal]
    momentum = [density * state[k] for k in (1, 2, 3)]
    square = state[1] * momentum[0] + state[2] * momentum[1] + state[3] * momentum[2]
    energy = pressure * (1.0 / (GAMMA - 1.0)) + 0.5 * square
    conserved = [density, *momentum, energy]
    flux = [momentum[normal - 1]]
    for k in range(3):
        term = speed * momentum[k]
        flux.append(term + pressure if k == normal - 1 else term)
    flux.append(speed * (energy + pressure))
    return conserved, flux, jnp.abs(speed) + jnp.sqrt(GAMMA * pressure / density)


def flux_difference(cells, axis, normal):
    states, _ = primitives(cells)
    faces = [rebuild(profile, axis) for profile in states]
    left = face_terms([pair[0] for pair in faces], normal)
    right = face_terms([pair[1] for pair in faces], normal)
    signal = 0.5 * jnp.maximum(left[2], right[2])
    differences = []
    for k in range(FIELDS):
        flux = 0.5 * (left[1][k] + right[1][k]) - signal * (right[0][k] - left[0][k])
        differences.append(flux - shifted(flux, -1, axis))
    return differences


def start_kernel(fields_ref, peak_ref, first_ref, last_ref):
    rows = fields_ref.shape[1]
    for k in range(FIELDS):
        first_ref[k * WIDTH : (k + 1) * WIDTH, :] = fields_ref[k, :WIDTH, :]
        last_ref[k * WIDTH : (k + 1) * WIDTH, :] = fields_ref[k, rows - WIDTH :, :]
    first_ref[FIELDS * WIDTH :, :] = fields_ref[0, :1, :]
    last_ref[FIELDS * WIDTH :, :] = fields_ref[0, :1, :]
    (density, *velocity, pressure), _ = primitives([fields_ref[k] for k in range(FIELDS)])
    speed = jnp.maximum(jnp.abs(velocity[0]), jnp.abs(velocity[1]))
    speed = speed + jnp.sqrt(GAMMA * pressure / density)
    peak = jnp.max(speed, axis=0, keepdims=True)
    peak_ref[...] = jnp.broadcast_to(peak[None], peak_ref.shape)


def extended_rows(fields_ref, before_ref, after_ref, full_ref):
    rows = fields_ref.shape[1]
    for k in range(FIELDS):
        full_ref[k, :rows, :] = fields_ref[k]
        full_ref[k, rows : rows + 8, :] = fields_ref[k, :8, :]
        full_ref[k, rows : rows + WIDTH, :] = after_ref[k * WIDTH : (k + 1) * WIDTH, :]
        full_ref[k, rows + 8 - WIDTH : rows + 8, :] = before_ref[k * WIDTH : (k + 1) * WIDTH, :]


def pack_kernel(fields_ref, before_ref, after_ref, full_ref, own_ref):
    rows, columns = fields_ref.shape[1:]
    extended_rows(fields_ref, before_ref, after_ref, full_ref)
    lane = lax.broadcasted_iota(jnp.int32, (rows + 8, columns), 1)
    packed = jnp.zeros((rows + 8, columns), jnp.float32)
    for k in range(FIELDS):
        at = k * 4 * WIDTH
        ends = pltpu.roll(full_ref[k], at + 2 * WIDTH, 1)
        packed = jnp.where((lane >= at) & (lane < at + 4 * WIDTH), ends, packed)
    pad = jnp.zeros((columns - rows - 8, columns), jnp.float32)
    own_ref[...] = jnp.transpose(jnp.concatenate([packed, pad], axis=0))[: own_ref.shape[0]]


def fill_kernel(me_ref, peaks_ref, own_ref, send_ref):
    count = send_ref.shape[0]
    before = lax.rem(me_ref[0] + count - 1, count)
    peak = jnp.max(peaks_ref[...], axis=0)
    for j in range(count):
        send_ref[j, PACKED - 1 :, :] = peak
        for k in range(FIELDS):
            at = k * 4 * WIDTH + WIDTH
            send_ref[j, k * WIDTH : (k + 1) * WIDTH, :] = own_ref[at : at + WIDTH, :]
    for k in range(FIELDS):
        at = k * 4 * WIDTH + 2 * WIDTH
        send_ref[before, k * WIDTH : (k + 1) * WIDTH, :] = own_ref[at : at + WIDTH, :]


def inner_kernel(full_ref, change_ref):
    for row in range(0, full_ref.shape[1], 8):
        change = flux_difference([full_ref[k, row : row + 8, :] for k in range(FIELDS)], 1, 1)
        for k in range(FIELDS):
            change_ref[k, row : row + 8, :] = change[k]


def sweep_kernel(me_ref, full_ref, change_ref, own_ref, received_ref, out_ref, strip_ref, turned_ref):
    count = received_ref.shape[0]
    rows, columns = out_ref.shape[1:]
    me = me_ref[0]
    before, after = lax.rem(me + count - 1, count), lax.rem(me + 1, count)
    peak = jnp.max(received_ref[:, PACKED - 1, :], axis=0, keepdims=True)
    time_step = COURANT / jnp.max(peak, axis=1, keepdims=True)
    for k in range(FIELDS):
        at, own = k * WIDTH, k * 4 * WIDTH
        strip_ref[k, :6, :] = own_ref[own : own + 6, :]
        strip_ref[k, 6:9, :] = received_ref[after, at : at + WIDTH, :]
        strip_ref[k, 9:12, :] = received_ref[before, at : at + WIDTH, :]
        strip_ref[k, 12:18, :] = own_ref[own + 6 : own + 12, :]
        strip_ref[k, 18:, :] = own_ref[own : own + 6, :]
    edge = flux_difference([strip_ref[k] for k in range(FIELDS)], 0, 1)
    turned_ref[...] = jnp.zeros_like(turned_ref)
    for k in range(FIELDS):
        turned_ref[6 * k : 6 * k + 3, :] = edge[k][3:6]
        turned_ref[6 * k + 3 : 6 * k + 6, :] = edge[k][12:15]
    turned = jnp.transpose(turned_ref[...])[: rows + 8]
    lane = lax.broadcasted_iota(jnp.int32, (rows + 8, columns), 1)
    at_edge = (lane < WIDTH) | (lane >= columns - WIDTH)
    cells = []
    for k in range(FIELDS):
        sides = pltpu.roll(turned, columns - WIDTH - 6 * k, 1)
        change = jnp.where(at_edge, sides, change_ref[k])
        cells.append(full_ref[k] - time_step * change)
    change = flux_difference(cells, 0, 2)
    for k in range(FIELDS):
        out_ref[k] = (cells[k] - time_step * change[k])[:rows]


def call(kernel, out_shape, n_smem, n_vmem, scratch=()):
    return pl.pallas_call(
        kernel,
        out_shape=out_shape,
        in_specs=[SMEM] * n_smem + [VMEM] * n_vmem,
        out_specs=jax.tree.map(lambda _: VMEM, out_shape),
        scratch_shapes=list(scratch),
        cost_estimate=pl.CostEstimate(flops=4_000_000, bytes_accessed=1_000_000, transcendentals=0),
    )


def f32(*shape):
    return jax.ShapeDtypeStruct(shape, jnp.float32)


def kept(*shape):
    return pltpu.VMEM(shape, jnp.float32)


def held(*arrays):
    return [pltpu.with_memory_space_constraint(array, pltpu.VMEM) for array in arrays]


def local(fields):
    rows, columns = fields.shape[2:]
    cells = fields.reshape(FIELDS, rows, columns)
    count_row, count_col = lax.axis_size(ROW), lax.axis_size(COL)
    me = lax.axis_index(ROW).astype(jnp.int32).reshape(1)
    full = (FIELDS, rows + 8, columns)
    packed = kept(PACKED, columns)
    own = kept(64, columns)
    up = [(i, (i + 1) % count_col) for i in range(count_col)]

    shapes = (kept(count_col, 1, columns), packed, packed)
    peaks, first, last = call(start_kernel, shapes, 0, 1)(cells)
    before = lax.ppermute(last, COL, up)
    after = lax.ppermute(first, COL, [(j, i) for i, j in up])
    peaks = lax.all_to_all(peaks, COL, 0, 0, tiled=True)
    grown, own = call(pack_kernel, (kept(*full), own), 0, 3)(cells, *held(before, after))
    send = call(fill_kernel, kept(count_row, PACKED, columns), 1, 2)(me, *held(peaks, own))
    received = lax.all_to_all(send, ROW, 0, 0, tiled=True)
    change = call(inner_kernel, kept(*full), 0, 1)(*held(grown))
    scratch = [pltpu.VMEM((FIELDS, 24, columns), jnp.float32), pltpu.VMEM((columns, columns), jnp.float32)]
    out = call(sweep_kernel, f32(FIELDS, rows, columns), 1, 4, scratch)(
        me, *held(grown, change, own, received)
    )
    return out.reshape(fields.shape)


def solution(mesh):
    split = Mesh(mesh.devices.reshape(8, 2, 8, 4, 2), (*ROW, *COL))
    placed = (P(None, None, COL, ROW),)
    return jax.shard_map(
        local, mesh=split, in_specs=placed, out_specs=P(None, None, COL, ROW), check_vma=False
    )
```

```python
import jax
import jax.numpy as jnp
from jax import lax
from jax.experimental import pallas as pl
from jax.experimental.pallas import tpu as pltpu
from jax.sharding import Mesh
from jax.sharding import PartitionSpec as P

ROW = ("row_0", "row_1")
COL = ("col_0", "col_1", "col_2")

GAMMA = 1.4
COURANT = 0.3
WIDTH = 3
FIELDS = 5
PACKED = 8
STRIP = 9
VMEM = pl.BlockSpec(memory_space=pltpu.VMEM)
SMEM = pl.BlockSpec(memory_space=pltpu.SMEM)


def minmod(first, second):
    low = jnp.minimum(first, second)
    high = jnp.maximum(first, second)
    return jnp.maximum(low, 0.0) + jnp.minimum(high, 0.0)


def shifted(profile, step, axis):
    return pltpu.roll(profile, (-step) % profile.shape[axis], axis)


def primitives(cells):
    inverse = 1.0 / cells[0]
    velocity = [cells[k] * inverse for k in (1, 2, 3)]
    kinetic = 0.5 * (cells[1] * velocity[0] + cells[2] * velocity[1] + cells[3] * velocity[2])
    return [cells[0], *velocity, (GAMMA - 1.0) * (cells[4] - kinetic)], inverse


def rebuild(profile, axis):
    after = shifted(profile, 1, axis)
    edge = 7.0 / 12.0 * (profile + after) - 1.0 / 12.0 * (
        shifted(profile, -1, axis) + shifted(profile, 2, axis)
    )
    edge = jnp.clip(edge, jnp.minimum(profile, after), jnp.maximum(profile, after))
    rise = edge - profile
    fall = profile - shifted(edge, -1, axis)
    right = profile + minmod(rise, 2.0 * fall)
    left = profile - minmod(fall, 2.0 * rise)
    return right, shifted(left, 1, axis)


def face_terms(state, normal):
    density, pressure = state[0], state[4]
    speed = state[normal]
    momentum = [density * state[k] for k in (1, 2, 3)]
    square = state[1] * momentum[0] + state[2] * momentum[1] + state[3] * momentum[2]
    energy = pressure * (1.0 / (GAMMA - 1.0)) + 0.5 * square
    conserved = [density, *momentum, energy]
    flux = [momentum[normal - 1]]
    for k in range(3):
        term = speed * momentum[k]
        flux.append(term + pressure if k == normal - 1 else term)
    flux.append(speed * (energy + pressure))
    return conserved, flux, jnp.abs(speed) + jnp.sqrt(GAMMA * pressure / density)


def flux_difference(cells, axis, normal):
    states, _ = primitives(cells)
    faces = [rebuild(profile, axis) for profile in states]
    left = face_terms([pair[0] for pair in faces], normal)
    right = face_terms([pair[1] for pair in faces], normal)
    signal = 0.5 * jnp.maximum(left[2], right[2])
    differences = []
    for k in range(FIELDS):
        flux = 0.5 * (left[1][k] + right[1][k]) - signal * (right[0][k] - left[0][k])
        differences.append(flux - shifted(flux, -1, axis))
    return differences


def start_kernel(me_ref, fields_ref, send_ref, own_ref, cells_ref, swapped_ref):
    count = send_ref.shape[0]
    rows, columns = fields_ref.shape[1:]
    cells = [fields_ref[k] for k in range(FIELDS)]
    for k in range(FIELDS):
        cells_ref[k] = cells[k]
    (density, *velocity, pressure), _ = primitives(cells)
    speed = jnp.maximum(jnp.abs(velocity[0]), jnp.abs(velocity[1]))
    speed = speed + jnp.sqrt(GAMMA * pressure / density)
    peak = jnp.max(speed, axis=0, keepdims=True)
    peak = jnp.maximum(peak, pltpu.roll(peak, rows, 1))
    lane = lax.broadcasted_iota(jnp.int32, (rows, columns), 1)
    ends = starts = jnp.zeros((rows, columns), jnp.float32)
    for k in range(FIELDS):
        at = k * STRIP
        turned = pltpu.roll(cells[k], at + 2 * WIDTH, 1)
        ends = jnp.where((lane >= at) & (lane < at + 2 * WIDTH), turned, ends)
        turned = pltpu.roll(cells[k], at + WIDTH, 1)
        starts = jnp.where((lane >= at + WIDTH) & (lane < at + STRIP), turned, starts)
    own = jnp.transpose(jnp.concatenate([ends, starts], axis=0))[: own_ref.shape[0]]
    own_ref[...] = own
    swapped_ref[...] = pltpu.roll(own, rows, 1)
    half = lax.broadcasted_iota(jnp.int32, (1, columns), 1) < rows

    def row_of(ref, slot):
        at = slot // WIDTH * STRIP + WIDTH + slot % WIDTH
        return ref[at : at + 1, :]

    ends, starts = [], []
    for row in range(PACKED):
        last = row == PACKED - 1
        ends.append(
            jnp.where(half, row_of(own_ref, row), peak if last else row_of(swapped_ref, PACKED + row))
        )
        starts.append(
            jnp.where(half, row_of(swapped_ref, row), peak if last else row_of(own_ref, PACKED + row))
        )
    ends, starts = jnp.concatenate(ends, axis=0), jnp.concatenate(starts, axis=0)
    for j in range(count):
        send_ref[j] = ends
    send_ref[lax.rem(me_ref[0] + count - 1, count)] = starts


def inner_kernel(cells_ref, change_ref):
    for row in range(0, cells_ref.shape[1], 8):
        change = flux_difference([cells_ref[k, row : row + 8, :] for k in range(FIELDS)], 1, 1)
        for k in range(FIELDS):
            change_ref[k, row : row + 8, :] = change[k]


def edge_kernel(
    me_ref, cells_ref, inner_ref, own_ref, received_ref,
    change_ref, first_ref, last_ref, peak_ref, strip_ref, side_ref, turned_ref,
):
    count = received_ref.shape[0]
    rows, columns = cells_ref.shape[1:]
    me = me_ref[0]
    before, after = lax.rem(me + count - 1, count), lax.rem(me + 1, count)
    half = lax.broadcasted_iota(jnp.int32, (1, columns), 1) < rows
    peak = jnp.max(received_ref[:, PACKED - 1, :], axis=0, keepdims=True)
    peak = jnp.where(half, pltpu.roll(peak, rows, 1), peak)
    peak_ref[...] = jnp.broadcast_to(peak[None], peak_ref.shape)

    side_ref[0] = received_ref[after]
    side_ref[1] = pltpu.roll(received_ref[after], rows, 1)
    side_ref[2] = received_ref[before]
    side_ref[3] = pltpu.roll(received_ref[before], rows, 1)
    for k in range(FIELDS):
        at = k * STRIP
        strip_ref[k, :STRIP, :] = own_ref[at : at + STRIP, :]
        strip_ref[k, STRIP:, :] = jnp.broadcast_to(own_ref[at + WIDTH : at + WIDTH + 1, :], (16 - STRIP, columns))
        for j in range(WIDTH):
            slot = k * WIDTH + j
            row, far = slot % PACKED, slot // PACKED
            low, high = at + j, at + 2 * WIDTH + j
            strip_ref[k, j : j + 1, :] = jnp.where(
                half, own_ref[low : low + 1, :], side_ref[2 if far else 3, row : row + 1, :]
            )
            strip_ref[k, 2 * WIDTH + j : 2 * WIDTH + j + 1, :] = jnp.where(
                half, side_ref[1 if far else 0, row : row + 1, :], own_ref[high : high + 1, :]
            )
    edge = flux_difference([strip_ref[k] for k in range(FIELDS)], 0, 1)
    turned_ref[...] = jnp.zeros_like(turned_ref)
    for k in range(FIELDS):
        turned_ref[k * WIDTH : (k + 1) * WIDTH, :] = edge[k][WIDTH : 2 * WIDTH]
    turned = jnp.transpose(turned_ref[...])
    at_end, at_start = turned[:rows], turned[rows:]
    lane = lax.broadcasted_iota(jnp.int32, (rows, columns), 1)
    for k in range(FIELDS):
        change = jnp.where(
            lane >= columns - WIDTH, pltpu.roll(at_end, columns - WIDTH - k * WIDTH, 1), inner_ref[k]
        )
        change = jnp.where(lane < WIDTH, pltpu.roll(at_start, (-k * WIDTH) % columns, 1), change)
        change_ref[k] = change
        at, far = k * WIDTH, (FIELDS + k) * WIDTH
        first_ref[at : at + WIDTH, :] = cells_ref[k, :WIDTH, :]
        last_ref[at : at + WIDTH, :] = cells_ref[k, rows - WIDTH :, :]
        first_ref[far : far + WIDTH, :] = change[:WIDTH]
        last_ref[far : far + WIDTH, :] = change[rows - WIDTH :]
    first_ref[2 * FIELDS * WIDTH :, :] = jnp.zeros((2, columns), jnp.float32)
    last_ref[2 * FIELDS * WIDTH :, :] = jnp.zeros((2, columns), jnp.float32)


def sweep_kernel(cells_ref, change_ref, peaks_ref, before_ref, after_ref, out_ref, half_ref):
    rows, columns = out_ref.shape[1:]
    peak = jnp.max(jnp.max(peaks_ref[...], axis=0), axis=1, keepdims=True)
    time_step = COURANT / peak
    size = FIELDS * WIDTH
    before = before_ref[:size, :] - time_step * before_ref[size : 2 * size, :]
    after = after_ref[:size, :] - time_step * after_ref[size : 2 * size, :]
    for k in range(FIELDS):
        half = cells_ref[k] - time_step * change_ref[k]
        half_ref[k, :rows, :] = half
        half_ref[k, rows : rows + 8, :] = half[:8]
        half_ref[k, rows : rows + WIDTH, :] = after[k * WIDTH : (k + 1) * WIDTH]
        half_ref[k, rows + 8 - WIDTH : rows + 8, :] = before[k * WIDTH : (k + 1) * WIDTH]
    cells = [half_ref[k] for k in range(FIELDS)]
    change = flux_difference(cells, 0, 2)
    for k in range(FIELDS):
        out_ref[k] = (cells[k] - time_step * change[k])[:rows]


def call(kernel, out_shape, n_smem, n_vmem, scratch=()):
    return pl.pallas_call(
        kernel,
        out_shape=out_shape,
        in_specs=[SMEM] * n_smem + [VMEM] * n_vmem,
        out_specs=jax.tree.map(lambda _: VMEM, out_shape),
        scratch_shapes=list(scratch),
        cost_estimate=pl.CostEstimate(flops=4_000_000, bytes_accessed=1_000_000, transcendentals=0),
    )


def f32(*shape):
    return jax.ShapeDtypeStruct(shape, jnp.float32)


def kept(*shape):
    return pltpu.VMEM(shape, jnp.float32)


def held(*arrays):
    return [pltpu.with_memory_space_constraint(array, pltpu.VMEM) for array in arrays]


def local(fields):
    rows, columns = fields.shape[2:]
    fields = fields.reshape(FIELDS, rows, columns)
    count_row, count_col = lax.axis_size(ROW), lax.axis_size(COL)
    me = lax.axis_index(ROW).astype(jnp.int32).reshape(1)
    whole = kept(FIELDS, rows, columns)
    halo = kept(32, columns)
    up = [(i, (i + 1) % count_col) for i in range(count_col)]

    shapes = (kept(count_row, PACKED, columns), kept(48, columns), whole)
    send, own, cells = call(start_kernel, shapes, 1, 1, [pltpu.VMEM((48, columns), jnp.float32)])(me, fields)
    received = lax.all_to_all(send, ROW, 0, 0, tiled=True)
    inner = call(inner_kernel, whole, 0, 1)(*held(cells))
    shapes = (whole, halo, halo, kept(count_col, 1, columns))
    scratch = [(FIELDS, 16, columns), (4, PACKED, columns), (columns, columns)]
    scratch = [pltpu.VMEM(shape, jnp.float32) for shape in scratch]
    change, first, last, peak = call(edge_kernel, shapes, 1, 4, scratch)(
        me, *held(cells, inner, own, received)
    )
    peaks = lax.all_to_all(peak, COL, 0, 0, tiled=True)
    before = lax.ppermute(last, COL, up)
    after = lax.ppermute(first, COL, [(j, i) for i, j in up])
    scratch = [pltpu.VMEM((FIELDS, rows + 8, columns), jnp.float32)]
    out = call(sweep_kernel, f32(FIELDS, rows, columns), 0, 5, scratch)(
        *held(cells, change, peaks, before, after)
    )
    return out.reshape(FIELDS, 1, rows, columns)


def solution(mesh):
    split = Mesh(mesh.devices.reshape(8, 2, 8, 4, 2), (*ROW, *COL))
    placed = (P(None, None, COL, ROW),)
    return jax.shard_map(
        local, mesh=split, in_specs=placed, out_specs=P(None, None, COL, ROW), check_vma=False
    )
```

```python
import jax
import jax.numpy as jnp
from jax import lax
from jax.experimental import pallas as pl
from jax.experimental.pallas import tpu as pltpu
from jax.sharding import Mesh
from jax.sharding import PartitionSpec as P

ROW = ("row_0", "row_1")
COL = ("col_0", "col_1", "col_2")

GAMMA = 1.4
COURANT = 0.3
WIDTH = 3
FIELDS = 5
PACKED = 8
STRIP = 9
VMEM = pl.BlockSpec(memory_space=pltpu.VMEM)
SMEM = pl.BlockSpec(memory_space=pltpu.SMEM)


def minmod(first, second):
    low = jnp.minimum(first, second)
    high = jnp.maximum(first, second)
    return jnp.maximum(low, 0.0) + jnp.minimum(high, 0.0)


def shifted(profile, step, axis):
    return pltpu.roll(profile, (-step) % profile.shape[axis], axis)


def primitives(cells):
    inverse = 1.0 / cells[0]
    velocity = [cells[k] * inverse for k in (1, 2, 3)]
    kinetic = 0.5 * (cells[1] * velocity[0] + cells[2] * velocity[1] + cells[3] * velocity[2])
    return [cells[0], *velocity, (GAMMA - 1.0) * (cells[4] - kinetic)], inverse


def rebuild(profile, axis):
    after = shifted(profile, 1, axis)
    edge = 7.0 / 12.0 * (profile + after) - 1.0 / 12.0 * (
        shifted(profile, -1, axis) + shifted(profile, 2, axis)
    )
    edge = jnp.clip(edge, jnp.minimum(profile, after), jnp.maximum(profile, after))
    rise = edge - profile
    fall = profile - shifted(edge, -1, axis)
    right = profile + minmod(rise, 2.0 * fall)
    left = profile - minmod(fall, 2.0 * rise)
    return right, shifted(left, 1, axis)


def face_terms(state, normal):
    density, pressure = state[0], state[4]
    speed = state[normal]
    momentum = [density * state[k] for k in (1, 2, 3)]
    square = state[1] * momentum[0] + state[2] * momentum[1] + state[3] * momentum[2]
    energy = pressure * (1.0 / (GAMMA - 1.0)) + 0.5 * square
    conserved = [density, *momentum, energy]
    flux = [momentum[normal - 1]]
    for k in range(3):
        term = speed * momentum[k]
        flux.append(term + pressure if k == normal - 1 else term)
    flux.append(speed * (energy + pressure))
    return conserved, flux, jnp.abs(speed) + jnp.sqrt(GAMMA * pressure / density)


def flux_difference(cells, axis, normal):
    states, _ = primitives(cells)
    faces = [rebuild(profile, axis) for profile in states]
    left = face_terms([pair[0] for pair in faces], normal)
    right = face_terms([pair[1] for pair in faces], normal)
    signal = 0.5 * jnp.maximum(left[2], right[2])
    differences = []
    for k in range(FIELDS):
        flux = 0.5 * (left[1][k] + right[1][k]) - signal * (right[0][k] - left[0][k])
        differences.append(flux - shifted(flux, -1, axis))
    return differences


def start_kernel(me_ref, fields_ref, send_ref, own_ref, cells_ref, swapped_ref):
    count = send_ref.shape[0]
    rows, columns = fields_ref.shape[1:]
    cells = [fields_ref[k] for k in range(FIELDS)]
    for k in range(FIELDS):
        cells_ref[k] = cells[k]
    (density, *velocity, pressure), _ = primitives(cells)
    speed = jnp.maximum(jnp.abs(velocity[0]), jnp.abs(velocity[1]))
    speed = speed + jnp.sqrt(GAMMA * pressure / density)
    peak = jnp.max(speed, axis=0, keepdims=True)
    peak = jnp.maximum(peak, pltpu.roll(peak, rows, 1))
    lane = lax.broadcasted_iota(jnp.int32, (rows, columns), 1)
    ends = starts = jnp.zeros((rows, columns), jnp.float32)
    for k in range(FIELDS):
        at = k * STRIP
        turned = pltpu.roll(cells[k], at + 2 * WIDTH, 1)
        ends = jnp.where((lane >= at) & (lane < at + 2 * WIDTH), turned, ends)
        turned = pltpu.roll(cells[k], at + WIDTH, 1)
        starts = jnp.where((lane >= at + WIDTH) & (lane < at + STRIP), turned, starts)
    own = jnp.transpose(jnp.concatenate([ends, starts], axis=0))[: own_ref.shape[0]]
    own_ref[...] = own
    swapped_ref[...] = pltpu.roll(own, rows, 1)
    half = lax.broadcasted_iota(jnp.int32, (1, columns), 1) < rows

    def row_of(ref, slot):
        at = slot // WIDTH * STRIP + WIDTH + slot % WIDTH
        return ref[at : at + 1, :]

    ends, starts = [], []
    for row in range(PACKED):
        last = row == PACKED - 1
        ends.append(
            jnp.where(half, row_of(own_ref, row), peak if last else row_of(swapped_ref, PACKED + row))
        )
        starts.append(
            jnp.where(half, row_of(swapped_ref, row), peak if last else row_of(own_ref, PACKED + row))
        )
    ends, starts = jnp.concatenate(ends, axis=0), jnp.concatenate(starts, axis=0)
    for j in range(count):
        send_ref[j] = ends
    send_ref[lax.rem(me_ref[0] // 2 + count - 1, count)] = starts


def inner_kernel(cells_ref, change_ref):
    for row in range(0, cells_ref.shape[1], 8):
        change = flux_difference([cells_ref[k, row : row + 8, :] for k in range(FIELDS)], 1, 1)
        for k in range(FIELDS):
            change_ref[k, row : row + 8, :] = change[k]


def edge_kernel(
    me_ref, cells_ref, inner_ref, own_ref, received_ref,
    change_ref, near_ref, far_ref, peak_ref, strip_ref, side_ref, turned_ref,
):
    count = received_ref.shape[0]
    rows, columns = cells_ref.shape[1:]
    me, odd = me_ref[0] // 2, lax.rem(me_ref[0], 2) == 1
    before, after = lax.rem(me + count - 1, count), lax.rem(me + 1, count)
    half = lax.broadcasted_iota(jnp.int32, (1, columns), 1) < rows
    peak = jnp.max(received_ref[:, PACKED - 1, :], axis=0, keepdims=True)
    peak = jnp.where(half, pltpu.roll(peak, rows, 1), peak)
    peak_ref[...] = jnp.broadcast_to(peak[None], peak_ref.shape)

    side_ref[0] = received_ref[after]
    side_ref[1] = pltpu.roll(received_ref[after], rows, 1)
    side_ref[2] = received_ref[before]
    side_ref[3] = pltpu.roll(received_ref[before], rows, 1)
    for k in range(FIELDS):
        at = k * STRIP
        strip_ref[k, :STRIP, :] = own_ref[at : at + STRIP, :]
        strip_ref[k, STRIP:, :] = jnp.broadcast_to(own_ref[at + WIDTH : at + WIDTH + 1, :], (16 - STRIP, columns))
        for j in range(WIDTH):
            slot = k * WIDTH + j
            row, far = slot % PACKED, slot // PACKED
            low, high = at + j, at + 2 * WIDTH + j
            strip_ref[k, j : j + 1, :] = jnp.where(
                half, own_ref[low : low + 1, :], side_ref[2 if far else 3, row : row + 1, :]
            )
            strip_ref[k, 2 * WIDTH + j : 2 * WIDTH + j + 1, :] = jnp.where(
                half, side_ref[1 if far else 0, row : row + 1, :], own_ref[high : high + 1, :]
            )
    edge = flux_difference([strip_ref[k] for k in range(FIELDS)], 0, 1)
    turned_ref[...] = jnp.zeros_like(turned_ref)
    for k in range(FIELDS):
        turned_ref[k * WIDTH : (k + 1) * WIDTH, :] = edge[k][WIDTH : 2 * WIDTH]
    turned = jnp.transpose(turned_ref[...])
    at_end, at_start = turned[:rows], turned[rows:]
    lane = lax.broadcasted_iota(jnp.int32, (rows, columns), 1)
    for k in range(FIELDS):
        change = jnp.where(
            lane >= columns - WIDTH, pltpu.roll(at_end, columns - WIDTH - k * WIDTH, 1), inner_ref[k]
        )
        change = jnp.where(lane < WIDTH, pltpu.roll(at_start, (-k * WIDTH) % columns, 1), change)
        change_ref[k] = change
        ends = [(cells_ref[k, :WIDTH, :], cells_ref[k, rows - WIDTH :, :]), (change[:WIDTH], change[rows - WIDTH :])]
        for part, (first, last) in enumerate(ends):
            at = (part * FIELDS + k) * WIDTH
            near_ref[at : at + WIDTH, :] = jnp.where(odd, first, last)
            far_ref[at : at + WIDTH, :] = jnp.where(odd, last, first)
    near_ref[2 * FIELDS * WIDTH :, :] = jnp.zeros((2, columns), jnp.float32)
    far_ref[2 * FIELDS * WIDTH :, :] = jnp.zeros((2, columns), jnp.float32)


def sweep_kernel(me_ref, cells_ref, change_ref, peaks_ref, near_ref, far_ref, out_ref, half_ref):
    rows, columns = out_ref.shape[1:]
    peak = jnp.max(jnp.max(peaks_ref[...], axis=0), axis=1, keepdims=True)
    time_step = COURANT / peak
    size = FIELDS * WIDTH
    odd = lax.rem(me_ref[0], 2) == 1
    near = near_ref[:size, :] - time_step * near_ref[size : 2 * size, :]
    far = far_ref[:size, :] - time_step * far_ref[size : 2 * size, :]
    before, after = jnp.where(odd, near, far), jnp.where(odd, far, near)
    for k in range(FIELDS):
        half = cells_ref[k] - time_step * change_ref[k]
        half_ref[k, :rows, :] = half
        half_ref[k, rows : rows + 8, :] = half[:8]
        half_ref[k, rows : rows + WIDTH, :] = after[k * WIDTH : (k + 1) * WIDTH]
        half_ref[k, rows + 8 - WIDTH : rows + 8, :] = before[k * WIDTH : (k + 1) * WIDTH]
    cells = [half_ref[k] for k in range(FIELDS)]
    change = flux_difference(cells, 0, 2)
    for k in range(FIELDS):
        out_ref[k] = (cells[k] - time_step * change[k])[:rows]


def call(kernel, out_shape, n_smem, n_vmem, scratch=()):
    return pl.pallas_call(
        kernel,
        out_shape=out_shape,
        in_specs=[SMEM] * n_smem + [VMEM] * n_vmem,
        out_specs=jax.tree.map(lambda _: VMEM, out_shape),
        scratch_shapes=list(scratch),
        cost_estimate=pl.CostEstimate(flops=4_000_000, bytes_accessed=1_000_000, transcendentals=0),
    )


def f32(*shape):
    return jax.ShapeDtypeStruct(shape, jnp.float32)


def kept(*shape):
    return pltpu.VMEM(shape, jnp.float32)


def held(*arrays):
    return [pltpu.with_memory_space_constraint(array, pltpu.VMEM) for array in arrays]


def local(fields):
    rows, columns = fields.shape[2:]
    fields = fields.reshape(FIELDS, rows, columns)
    count_row, count_col = lax.axis_size(ROW), lax.axis_size(COL)
    me = (lax.axis_index(ROW) * 2 + lax.axis_index(COL[-1])).astype(jnp.int32).reshape(1)
    whole = kept(FIELDS, rows, columns)
    halo = kept(32, columns)
    inside = [(i, i ^ 1) for i in range(count_col)]
    between = [(i, (i + (1 if i % 2 else -1)) % count_col) for i in range(count_col)]

    shapes = (kept(count_row, PACKED, columns), kept(48, columns), whole)
    send, own, cells = call(start_kernel, shapes, 1, 1, [pltpu.VMEM((48, columns), jnp.float32)])(me, fields)
    received = lax.all_to_all(send, ROW, 0, 0, tiled=True)
    inner = call(inner_kernel, whole, 0, 1)(*held(cells))
    shapes = (whole, halo, halo, kept(count_col, 1, columns))
    scratch = [(FIELDS, 16, columns), (4, PACKED, columns), (columns, columns)]
    scratch = [pltpu.VMEM(shape, jnp.float32) for shape in scratch]
    change, near, far, peak = call(edge_kernel, shapes, 1, 4, scratch)(
        me, *held(cells, inner, own, received)
    )
    peaks = lax.all_to_all(peak, COL, 0, 0, tiled=True)
    far = lax.ppermute(far, COL, between)
    near = lax.ppermute(near, COL, inside)
    scratch = [pltpu.VMEM((FIELDS, rows + 8, columns), jnp.float32)]
    out = call(sweep_kernel, f32(FIELDS, rows, columns), 1, 5, scratch)(
        me, *held(cells, change, peaks, near, far)
    )
    return out.reshape(FIELDS, 1, rows, columns)


def solution(mesh):
    split = Mesh(mesh.devices.reshape(8, 2, 8, 4, 2), (*ROW, *COL))
    placed = (P(None, None, COL, ROW),)
    return jax.shard_map(
        local, mesh=split, in_specs=placed, out_specs=P(None, None, COL, ROW), check_vma=False
    )
```

```python
import jax
import jax.numpy as jnp
from jax import lax
from jax.experimental import pallas as pl
from jax.experimental.pallas import tpu as pltpu
from jax.sharding import Mesh
from jax.sharding import PartitionSpec as P


ROW = ("row_0", "row_1")
COL = ("col_0", "col_1", "col_2")

GAMMA = 1.4
COURANT = 0.3
WIDTH = 3
FIELDS = 5
PACKED = 8
STRIP = 9
VMEM = pl.BlockSpec(memory_space=pltpu.VMEM)
SMEM = pl.BlockSpec(memory_space=pltpu.SMEM)


def minmod(first, second):
    low = jnp.minimum(first, second)
    high = jnp.maximum(first, second)
    return jnp.maximum(low, 0.0) + jnp.minimum(high, 0.0)


def shifted(profile, step, axis):
    return pltpu.roll(profile, (-step) % profile.shape[axis], axis)


def primitives(cells):
    inverse = 1.0 / cells[0]
    velocity = [cells[k] * inverse for k in (1, 2, 3)]
    kinetic = 0.5 * (cells[1] * velocity[0] + cells[2] * velocity[1] + cells[3] * velocity[2])
    return [cells[0], *velocity, (GAMMA - 1.0) * (cells[4] - kinetic)], inverse


def rebuild(profile, axis):
    after = shifted(profile, 1, axis)
    edge = 7.0 / 12.0 * (profile + after) - 1.0 / 12.0 * (
        shifted(profile, -1, axis) + shifted(profile, 2, axis)
    )
    edge = jnp.clip(edge, jnp.minimum(profile, after), jnp.maximum(profile, after))
    rise = edge - profile
    fall = profile - shifted(edge, -1, axis)
    right = profile + minmod(rise, 2.0 * fall)
    left = profile - minmod(fall, 2.0 * rise)
    return right, shifted(left, 1, axis)


def face_terms(state, normal):
    density, pressure = state[0], state[4]
    speed = state[normal]
    momentum = [density * state[k] for k in (1, 2, 3)]
    square = state[1] * momentum[0] + state[2] * momentum[1] + state[3] * momentum[2]
    energy = pressure * (1.0 / (GAMMA - 1.0)) + 0.5 * square
    conserved = [density, *momentum, energy]
    flux = [momentum[normal - 1]]
    for k in range(3):
        term = speed * momentum[k]
        flux.append(term + pressure if k == normal - 1 else term)
    flux.append(speed * (energy + pressure))
    return conserved, flux, jnp.abs(speed) + jnp.sqrt(GAMMA * pressure / density)


def flux_difference(cells, axis, normal):
    states, _ = primitives(cells)
    faces = [rebuild(profile, axis) for profile in states]
    left = face_terms([pair[0] for pair in faces], normal)
    right = face_terms([pair[1] for pair in faces], normal)
    signal = 0.5 * jnp.maximum(left[2], right[2])
    differences = []
    for k in range(FIELDS):
        flux = 0.5 * (left[1][k] + right[1][k]) - signal * (right[0][k] - left[0][k])
        differences.append(flux - shifted(flux, -1, axis))
    return differences


def start_kernel(me_ref, fields_ref, send_ref, own_ref, cells_ref, swapped_ref):
    count = send_ref.shape[0]
    rows, columns = fields_ref.shape[1:]
    cells = [fields_ref[k] for k in range(FIELDS)]
    for k in range(FIELDS):
        cells_ref[k] = cells[k]
    (density, *velocity, pressure), _ = primitives(cells)
    speed = jnp.maximum(jnp.abs(velocity[0]), jnp.abs(velocity[1]))
    speed = speed + jnp.sqrt(GAMMA * pressure / density)
    peak = jnp.max(speed, axis=0, keepdims=True)
    peak = jnp.maximum(peak, pltpu.roll(peak, rows, 1))
    lane = lax.broadcasted_iota(jnp.int32, (rows, columns), 1)
    ends = starts = jnp.zeros((rows, columns), jnp.float32)
    for k in range(FIELDS):
        at = k * STRIP
        turned = pltpu.roll(cells[k], at + 2 * WIDTH, 1)
        ends = jnp.where((lane >= at) & (lane < at + 2 * WIDTH), turned, ends)
        turned = pltpu.roll(cells[k], at + WIDTH, 1)
        starts = jnp.where((lane >= at + WIDTH) & (lane < at + STRIP), turned, starts)
    own = jnp.transpose(jnp.concatenate([ends, starts], axis=0))[: own_ref.shape[0]]
    own_ref[...] = own
    swapped_ref[...] = pltpu.roll(own, rows, 1)
    half = lax.broadcasted_iota(jnp.int32, (1, columns), 1) < rows

    def row_of(ref, slot):
        at = slot // WIDTH * STRIP + WIDTH + slot % WIDTH
        return ref[at : at + 1, :]

    ends, starts = [], []
    for row in range(PACKED):
        last = row == PACKED - 1
        ends.append(
            jnp.where(half, row_of(own_ref, row), peak if last else row_of(swapped_ref, PACKED + row))
        )
        starts.append(
            jnp.where(half, row_of(swapped_ref, row), peak if last else row_of(own_ref, PACKED + row))
        )
    ends, starts = jnp.concatenate(ends, axis=0), jnp.concatenate(starts, axis=0)
    for j in range(count):
        send_ref[j] = ends
    send_ref[lax.rem(me_ref[0] // 2 + count - 1, count)] = starts


def inner_kernel(cells_ref, change_ref):
    for row in range(0, cells_ref.shape[1], 8):
        change = flux_difference([cells_ref[k, row : row + 8, :] for k in range(FIELDS)], 1, 1)
        for k in range(FIELDS):
            change_ref[k, row : row + 8, :] = change[k]


def peak_kernel(received_ref, peak_ref):
    columns = received_ref.shape[2]
    rows = columns // 2
    half = lax.broadcasted_iota(jnp.int32, (1, columns), 1) < rows
    peak = jnp.max(received_ref[...], axis=0)[PACKED - 1 :, :]
    peak = jnp.where(half, pltpu.roll(peak, rows, 1), peak)
    peak_ref[...] = jnp.broadcast_to(peak[None], peak_ref.shape)


def edge_kernel(
    me_ref, cells_ref, inner_ref, own_ref, received_ref,
    change_ref, near_ref, far_ref, strip_ref, side_ref, turned_ref,
):
    count = received_ref.shape[0]
    rows, columns = cells_ref.shape[1:]
    me, odd = me_ref[0] // 2, lax.rem(me_ref[0], 2) == 1
    before, after = lax.rem(me + count - 1, count), lax.rem(me + 1, count)
    half = lax.broadcasted_iota(jnp.int32, (1, columns), 1) < rows
    side_ref[0] = received_ref[after]
    side_ref[1] = pltpu.roll(received_ref[after], rows, 1)
    side_ref[2] = received_ref[before]
    side_ref[3] = pltpu.roll(received_ref[before], rows, 1)
    for k in range(FIELDS):
        at = k * STRIP
        strip_ref[k, :STRIP, :] = own_ref[at : at + STRIP, :]
        strip_ref[k, STRIP:, :] = jnp.broadcast_to(own_ref[at + WIDTH : at + WIDTH + 1, :], (16 - STRIP, columns))
        for j in range(WIDTH):
            slot = k * WIDTH + j
            row, far = slot % PACKED, slot // PACKED
            low, high = at + j, at + 2 * WIDTH + j
            strip_ref[k, j : j + 1, :] = jnp.where(
                half, own_ref[low : low + 1, :], side_ref[2 if far else 3, row : row + 1, :]
            )
            strip_ref[k, 2 * WIDTH + j : 2 * WIDTH + j + 1, :] = jnp.where(
                half, side_ref[1 if far else 0, row : row + 1, :], own_ref[high : high + 1, :]
            )
    edge = flux_difference([strip_ref[k] for k in range(FIELDS)], 0, 1)
    turned_ref[...] = jnp.zeros_like(turned_ref)
    for k in range(FIELDS):
        turned_ref[k * WIDTH : (k + 1) * WIDTH, :] = edge[k][WIDTH : 2 * WIDTH]
    turned = jnp.transpose(turned_ref[...])
    at_end, at_start = turned[:rows], turned[rows:]
    lane = lax.broadcasted_iota(jnp.int32, (rows, columns), 1)
    for k in range(FIELDS):
        change = jnp.where(
            lane >= columns - WIDTH, pltpu.roll(at_end, columns - WIDTH - k * WIDTH, 1), inner_ref[k]
        )
        change = jnp.where(lane < WIDTH, pltpu.roll(at_start, (-k * WIDTH) % columns, 1), change)
        change_ref[k] = change
        ends = [(cells_ref[k, :WIDTH, :], cells_ref[k, rows - WIDTH :, :]), (change[:WIDTH], change[rows - WIDTH :])]
        for part, (first, last) in enumerate(ends):
            at = (part * FIELDS + k) * WIDTH
            near_ref[at : at + WIDTH, :] = jnp.where(odd, first, last)
            far_ref[at : at + WIDTH, :] = jnp.where(odd, last, first)
    near_ref[2 * FIELDS * WIDTH :, :] = jnp.zeros((2, columns), jnp.float32)
    far_ref[2 * FIELDS * WIDTH :, :] = jnp.zeros((2, columns), jnp.float32)


def sweep_kernel(me_ref, cells_ref, change_ref, peaks_ref, near_ref, far_ref, out_ref, half_ref):
    rows, _ = out_ref.shape[1:]
    peak = jnp.max(jnp.max(peaks_ref[...], axis=0), axis=1, keepdims=True)
    time_step = COURANT / peak
    size = FIELDS * WIDTH
    odd = lax.rem(me_ref[0], 2) == 1
    near = near_ref[:size, :] - time_step * near_ref[size : 2 * size, :]
    far = far_ref[:size, :] - time_step * far_ref[size : 2 * size, :]
    before, after = jnp.where(odd, near, far), jnp.where(odd, far, near)
    for k in range(FIELDS):
        half = cells_ref[k] - time_step * change_ref[k]
        half_ref[k, :rows, :] = half
        half_ref[k, rows : rows + 8, :] = half[:8]
        half_ref[k, rows : rows + WIDTH, :] = after[k * WIDTH : (k + 1) * WIDTH]
        half_ref[k, rows + 8 - WIDTH : rows + 8, :] = before[k * WIDTH : (k + 1) * WIDTH]
    cells = [half_ref[k] for k in range(FIELDS)]
    change = flux_difference(cells, 0, 2)
    for k in range(FIELDS):
        out_ref[k] = (cells[k] - time_step * change[k])[:rows]


def call(kernel, out_shape, n_smem, n_vmem, scratch=()):
    return pl.pallas_call(
        kernel,
        out_shape=out_shape,
        in_specs=[SMEM] * n_smem + [VMEM] * n_vmem,
        out_specs=jax.tree.map(lambda _: VMEM, out_shape),
        scratch_shapes=list(scratch),
        cost_estimate=pl.CostEstimate(flops=4_000_000, bytes_accessed=1_000_000, transcendentals=0),
    )


def f32(*shape):
    return jax.ShapeDtypeStruct(shape, jnp.float32)


def kept(*shape):
    return pltpu.VMEM(shape, jnp.float32)


def held(*arrays):
    return [pltpu.with_memory_space_constraint(array, pltpu.VMEM) for array in arrays]


def local(fields):
    rows, columns = fields.shape[2:]
    fields = fields.reshape(FIELDS, rows, columns)
    count_row, count_col = lax.axis_size(ROW), lax.axis_size(COL)
    me = (lax.axis_index(ROW) * 2 + lax.axis_index(COL[-1])).astype(jnp.int32).reshape(1)
    whole = kept(FIELDS, rows, columns)
    halo = kept(32, columns)
    inside = [(i, i ^ 1) for i in range(count_col)]
    between = [(i, (i + (1 if i % 2 else -1)) % count_col) for i in range(count_col)]

    shapes = (kept(count_row, PACKED, columns), kept(48, columns), whole)
    scratch = [pltpu.VMEM((48, columns), jnp.float32)]
    send, own, cells = call(start_kernel, shapes, 1, 1, scratch)(me, fields)
    received = lax.all_to_all(send, ROW, 0, 0, tiled=True)
    inner = call(inner_kernel, whole, 0, 1)(*held(cells))
    peak = call(peak_kernel, kept(count_col, 1, columns), 0, 1)(*held(received))
    peaks = lax.all_to_all(peak, COL, 0, 0, tiled=True)
    scratch = [(FIELDS, 16, columns), (4, PACKED, columns), (columns, columns)]
    scratch = [pltpu.VMEM(shape, jnp.float32) for shape in scratch]
    change, near, far = call(edge_kernel, (whole, halo, halo), 1, 4, scratch)(me, *held(cells, inner, own, received))
    far = lax.ppermute(far, COL, between)
    near = lax.ppermute(near, COL, inside)
    scratch = [pltpu.VMEM((FIELDS, rows + 8, columns), jnp.float32)]
    out = call(sweep_kernel, f32(FIELDS, rows, columns), 1, 5, scratch)(
        me, *held(cells, change, peaks, near, far)
    )
    return out.reshape(FIELDS, 1, rows, columns)


def solution(mesh):
    split = Mesh(mesh.devices.reshape(8, 2, 8, 4, 2), (*ROW, *COL))
    placed = (P(None, None, COL, ROW),)
    return jax.shard_map(
        local, mesh=split, in_specs=placed, out_specs=P(None, None, COL, ROW), check_vma=False
    )
```

```python
import jax
import jax.numpy as jnp
from jax import lax
from jax.experimental import pallas as pl
from jax.experimental.pallas import tpu as pltpu
from jax.sharding import Mesh
from jax.sharding import PartitionSpec as P


ROW = ("row_0", "row_1")
COL = ("col_0", "col_1", "col_2")
SIDE = (*ROW, COL[-1])
REST = COL[:-1]

GAMMA = 1.4
COURANT = 0.3
WIDTH = 3
FIELDS = 5
PACKED = 8
STRIP = 9
VMEM = pl.BlockSpec(memory_space=pltpu.VMEM)
SMEM = pl.BlockSpec(memory_space=pltpu.SMEM)


def minmod(first, second):
    low = jnp.minimum(first, second)
    high = jnp.maximum(first, second)
    return jnp.maximum(low, 0.0) + jnp.minimum(high, 0.0)


def shifted(profile, step, axis):
    return pltpu.roll(profile, (-step) % profile.shape[axis], axis)


def primitives(cells):
    inverse = 1.0 / cells[0]
    velocity = [cells[k] * inverse for k in (1, 2, 3)]
    kinetic = 0.5 * (cells[1] * velocity[0] + cells[2] * velocity[1] + cells[3] * velocity[2])
    return [cells[0], *velocity, (GAMMA - 1.0) * (cells[4] - kinetic)], inverse


def rebuild(profile, axis):
    after = shifted(profile, 1, axis)
    edge = 7.0 / 12.0 * (profile + after) - 1.0 / 12.0 * (
        shifted(profile, -1, axis) + shifted(profile, 2, axis)
    )
    edge = jnp.clip(edge, jnp.minimum(profile, after), jnp.maximum(profile, after))
    rise = edge - profile
    fall = profile - shifted(edge, -1, axis)
    right = profile + minmod(rise, 2.0 * fall)
    left = profile - minmod(fall, 2.0 * rise)
    return right, shifted(left, 1, axis)


def face_terms(state, normal):
    density, pressure = state[0], state[4]
    speed = state[normal]
    momentum = [density * state[k] for k in (1, 2, 3)]
    square = state[1] * momentum[0] + state[2] * momentum[1] + state[3] * momentum[2]
    energy = pressure * (1.0 / (GAMMA - 1.0)) + 0.5 * square
    conserved = [density, *momentum, energy]
    flux = [momentum[normal - 1]]
    for k in range(3):
        term = speed * momentum[k]
        flux.append(term + pressure if k == normal - 1 else term)
    flux.append(speed * (energy + pressure))
    return conserved, flux, jnp.abs(speed) + jnp.sqrt(GAMMA * pressure / density)


def flux_difference(cells, axis, normal):
    states, _ = primitives(cells)
    faces = [rebuild(profile, axis) for profile in states]
    left = face_terms([pair[0] for pair in faces], normal)
    right = face_terms([pair[1] for pair in faces], normal)
    signal = 0.5 * jnp.maximum(left[2], right[2])
    differences = []
    for k in range(FIELDS):
        flux = 0.5 * (left[1][k] + right[1][k]) - signal * (right[0][k] - left[0][k])
        differences.append(flux - shifted(flux, -1, axis))
    return differences


def start_kernel(me_ref, fields_ref, send_ref, own_ref, cells_ref, swapped_ref):
    count = send_ref.shape[0]
    rows, columns = fields_ref.shape[1:]
    cells = [fields_ref[k] for k in range(FIELDS)]
    for k in range(FIELDS):
        cells_ref[k] = cells[k]
    (density, *velocity, pressure), _ = primitives(cells)
    speed = jnp.maximum(jnp.abs(velocity[0]), jnp.abs(velocity[1]))
    speed = speed + jnp.sqrt(GAMMA * pressure / density)
    peak = jnp.max(speed, axis=0, keepdims=True)
    peak = jnp.maximum(peak, pltpu.roll(peak, rows, 1))
    lane = lax.broadcasted_iota(jnp.int32, (rows, columns), 1)
    ends = starts = jnp.zeros((rows, columns), jnp.float32)
    for k in range(FIELDS):
        at = k * STRIP
        turned = pltpu.roll(cells[k], at + 2 * WIDTH, 1)
        ends = jnp.where((lane >= at) & (lane < at + 2 * WIDTH), turned, ends)
        turned = pltpu.roll(cells[k], at + WIDTH, 1)
        starts = jnp.where((lane >= at + WIDTH) & (lane < at + STRIP), turned, starts)
    own = jnp.transpose(jnp.concatenate([ends, starts], axis=0))[: own_ref.shape[0]]
    own_ref[...] = own
    swapped_ref[...] = pltpu.roll(own, rows, 1)
    half = lax.broadcasted_iota(jnp.int32, (1, columns), 1) < rows

    def row_of(ref, slot):
        at = slot // WIDTH * STRIP + WIDTH + slot % WIDTH
        return ref[at : at + 1, :]

    ends, starts = [], []
    for row in range(PACKED):
        last = row == PACKED - 1
        ends.append(
            jnp.where(half, row_of(own_ref, row), peak if last else row_of(swapped_ref, PACKED + row))
        )
        starts.append(
            jnp.where(half, row_of(swapped_ref, row), peak if last else row_of(own_ref, PACKED + row))
        )
    ends, starts = jnp.concatenate(ends, axis=0), jnp.concatenate(starts, axis=0)
    for j in range(count):
        send_ref[j] = ends
    send_ref[lax.rem(me_ref[0] + count - 2, count)] = starts


def inner_kernel(cells_ref, change_ref):
    for row in range(0, cells_ref.shape[1], 8):
        change = flux_difference([cells_ref[k, row : row + 8, :] for k in range(FIELDS)], 1, 1)
        for k in range(FIELDS):
            change_ref[k, row : row + 8, :] = change[k]


def peak_kernel(received_ref, peak_ref):
    columns = received_ref.shape[2]
    rows = columns // 2
    half = lax.broadcasted_iota(jnp.int32, (1, columns), 1) < rows
    peak = jnp.max(received_ref[...], axis=0)[PACKED - 1 :, :]
    peak = jnp.where(half, pltpu.roll(peak, rows, 1), peak)
    peak_ref[...] = jnp.broadcast_to(peak[None], peak_ref.shape)


def edge_kernel(
    me_ref, cells_ref, inner_ref, own_ref, received_ref,
    change_ref, near_ref, far_ref, strip_ref, side_ref, turned_ref,
):
    count = received_ref.shape[0]
    rows, columns = cells_ref.shape[1:]
    me, odd = me_ref[0], lax.rem(me_ref[0], 2) == 1
    before, after = lax.rem(me + count - 2, count), lax.rem(me + 2, count)
    half = lax.broadcasted_iota(jnp.int32, (1, columns), 1) < rows
    side_ref[0] = received_ref[after]
    side_ref[1] = pltpu.roll(received_ref[after], rows, 1)
    side_ref[2] = received_ref[before]
    side_ref[3] = pltpu.roll(received_ref[before], rows, 1)
    for k in range(FIELDS):
        at = k * STRIP
        strip_ref[k, :STRIP, :] = own_ref[at : at + STRIP, :]
        strip_ref[k, STRIP:, :] = jnp.broadcast_to(own_ref[at + WIDTH : at + WIDTH + 1, :], (16 - STRIP, columns))
        for j in range(WIDTH):
            slot = k * WIDTH + j
            row, far = slot % PACKED, slot // PACKED
            low, high = at + j, at + 2 * WIDTH + j
            strip_ref[k, j : j + 1, :] = jnp.where(
                half, own_ref[low : low + 1, :], side_ref[2 if far else 3, row : row + 1, :]
            )
            strip_ref[k, 2 * WIDTH + j : 2 * WIDTH + j + 1, :] = jnp.where(
                half, side_ref[1 if far else 0, row : row + 1, :], own_ref[high : high + 1, :]
            )
    edge = flux_difference([strip_ref[k] for k in range(FIELDS)], 0, 1)
    turned_ref[...] = jnp.zeros_like(turned_ref)
    for k in range(FIELDS):
        turned_ref[k * WIDTH : (k + 1) * WIDTH, :] = edge[k][WIDTH : 2 * WIDTH]
    turned = jnp.transpose(turned_ref[...])
    at_end, at_start = turned[:rows], turned[rows:]
    lane = lax.broadcasted_iota(jnp.int32, (rows, columns), 1)
    for k in range(FIELDS):
        change = jnp.where(
            lane >= columns - WIDTH, pltpu.roll(at_end, columns - WIDTH - k * WIDTH, 1), inner_ref[k]
        )
        change = jnp.where(lane < WIDTH, pltpu.roll(at_start, (-k * WIDTH) % columns, 1), change)
        change_ref[k] = change
        ends = [(cells_ref[k, :WIDTH, :], cells_ref[k, rows - WIDTH :, :]), (change[:WIDTH], change[rows - WIDTH :])]
        for part, (first, last) in enumerate(ends):
            at = (part * FIELDS + k) * WIDTH
            near_ref[at : at + WIDTH, :] = jnp.where(odd, first, last)
            far_ref[at : at + WIDTH, :] = jnp.where(odd, last, first)
    near_ref[2 * FIELDS * WIDTH :, :] = jnp.zeros((2, columns), jnp.float32)
    far_ref[2 * FIELDS * WIDTH :, :] = jnp.zeros((2, columns), jnp.float32)


def sweep_kernel(me_ref, cells_ref, change_ref, peaks_ref, near_ref, far_ref, out_ref, half_ref):
    rows, _ = out_ref.shape[1:]
    peak = jnp.max(jnp.max(peaks_ref[...], axis=0), axis=1, keepdims=True)
    time_step = COURANT / peak
    size = FIELDS * WIDTH
    odd = lax.rem(me_ref[0], 2) == 1
    near = near_ref[:size, :] - time_step * near_ref[size : 2 * size, :]
    far = far_ref[:size, :] - time_step * far_ref[size : 2 * size, :]
    before, after = jnp.where(odd, near, far), jnp.where(odd, far, near)
    for k in range(FIELDS):
        half = cells_ref[k] - time_step * change_ref[k]
        half_ref[k, :rows, :] = half
        half_ref[k, rows : rows + 8, :] = half[:8]
        half_ref[k, rows : rows + WIDTH, :] = after[k * WIDTH : (k + 1) * WIDTH]
        half_ref[k, rows + 8 - WIDTH : rows + 8, :] = before[k * WIDTH : (k + 1) * WIDTH]
    cells = [half_ref[k] for k in range(FIELDS)]
    change = flux_difference(cells, 0, 2)
    for k in range(FIELDS):
        out_ref[k] = (cells[k] - time_step * change[k])[:rows]


def call(kernel, out_shape, n_smem, n_vmem, scratch=()):
    return pl.pallas_call(
        kernel,
        out_shape=out_shape,
        in_specs=[SMEM] * n_smem + [VMEM] * n_vmem,
        out_specs=jax.tree.map(lambda _: VMEM, out_shape),
        scratch_shapes=list(scratch),
        cost_estimate=pl.CostEstimate(flops=4_000_000, bytes_accessed=1_000_000, transcendentals=0),
    )


def f32(*shape):
    return jax.ShapeDtypeStruct(shape, jnp.float32)


def kept(*shape):
    return pltpu.VMEM(shape, jnp.float32)


def held(*arrays):
    return [pltpu.with_memory_space_constraint(array, pltpu.VMEM) for array in arrays]


def local(fields):
    rows, columns = fields.shape[2:]
    fields = fields.reshape(FIELDS, rows, columns)
    count_side, count_rest, count_col = lax.axis_size(SIDE), lax.axis_size(REST), lax.axis_size(COL)
    me = lax.axis_index(SIDE).astype(jnp.int32).reshape(1)
    whole = kept(FIELDS, rows, columns)
    halo = kept(32, columns)
    inside = [(i, i ^ 1) for i in range(count_col)]
    between = [(i, (i + (1 if i % 2 else -1)) % count_col) for i in range(count_col)]

    shapes = (kept(count_side, PACKED, columns), kept(48, columns), whole)
    scratch = [pltpu.VMEM((48, columns), jnp.float32)]
    send, own, cells = call(start_kernel, shapes, 1, 1, scratch)(me, fields)
    received = lax.all_to_all(send, SIDE, 0, 0, tiled=True)
    inner = call(inner_kernel, whole, 0, 1)(*held(cells))
    peak = call(peak_kernel, kept(count_rest, 1, columns), 0, 1)(*held(received))
    peaks = lax.all_to_all(peak, REST, 0, 0, tiled=True)
    scratch = [(FIELDS, 16, columns), (4, PACKED, columns), (columns, columns)]
    scratch = [pltpu.VMEM(shape, jnp.float32) for shape in scratch]
    change, near, far = call(edge_kernel, (whole, halo, halo), 1, 4, scratch)(me, *held(cells, inner, own, received))
    far = lax.ppermute(far, COL, between)
    near = lax.ppermute(near, COL, inside)
    scratch = [pltpu.VMEM((FIELDS, rows + 8, columns), jnp.float32)]
    out = call(sweep_kernel, f32(FIELDS, rows, columns), 1, 5, scratch)(
        me, *held(cells, change, peaks, near, far)
    )
    return out.reshape(FIELDS, 1, rows, columns)


def solution(mesh):
    split = Mesh(mesh.devices.reshape(8, 2, 8, 4, 2), (*ROW, *COL))
    placed = (P(None, None, COL, ROW),)
    return jax.shard_map(
        local, mesh=split, in_specs=placed, out_specs=P(None, None, COL, ROW), check_vma=False
    )
```

```python
import functools

import jax
import jax.numpy as jnp
from jax import lax
from jax.experimental import pallas as pl
from jax.experimental.pallas import tpu as pltpu
from jax.sharding import Mesh
from jax.sharding import PartitionSpec as P


ROW = ("row_0", "row_1")
COL = ("col_0", "col_1", "col_2")
SIDE = (COL[-1], *ROW)
REST = (COL[1], COL[0])

GAMMA = 1.4
COURANT = 0.3
WIDTH = 3
FIELDS = 5
PACKED = 8
STRIP = 9
VMEM = pl.BlockSpec(memory_space=pltpu.VMEM)
SMEM = pl.BlockSpec(memory_space=pltpu.SMEM)


def minmod(first, second):
    low = jnp.minimum(first, second)
    high = jnp.maximum(first, second)
    return jnp.maximum(low, 0.0) + jnp.minimum(high, 0.0)


def shifted(profile, step, axis):
    return pltpu.roll(profile, (-step) % profile.shape[axis], axis)


def primitives(cells):
    inverse = 1.0 / cells[0]
    velocity = [cells[k] * inverse for k in (1, 2, 3)]
    kinetic = 0.5 * (cells[1] * velocity[0] + cells[2] * velocity[1] + cells[3] * velocity[2])
    return [cells[0], *velocity, (GAMMA - 1.0) * (cells[4] - kinetic)], inverse


def rebuild(profile, axis):
    after = shifted(profile, 1, axis)
    edge = 7.0 / 12.0 * (profile + after) - 1.0 / 12.0 * (
        shifted(profile, -1, axis) + shifted(profile, 2, axis)
    )
    edge = jnp.clip(edge, jnp.minimum(profile, after), jnp.maximum(profile, after))
    rise = edge - profile
    fall = profile - shifted(edge, -1, axis)
    right = profile + minmod(rise, 2.0 * fall)
    left = profile - minmod(fall, 2.0 * rise)
    return right, shifted(left, 1, axis)


def face_terms(state, normal):
    density, pressure = state[0], state[4]
    speed = state[normal]
    momentum = [density * state[k] for k in (1, 2, 3)]
    square = state[1] * momentum[0] + state[2] * momentum[1] + state[3] * momentum[2]
    energy = pressure * (1.0 / (GAMMA - 1.0)) + 0.5 * square
    conserved = [density, *momentum, energy]
    flux = [momentum[normal - 1]]
    for k in range(3):
        term = speed * momentum[k]
        flux.append(term + pressure if k == normal - 1 else term)
    flux.append(speed * (energy + pressure))
    return conserved, flux, jnp.abs(speed) + jnp.sqrt(GAMMA * pressure / density)


def flux_difference(cells, axis, normal):
    states, _ = primitives(cells)
    faces = [rebuild(profile, axis) for profile in states]
    left = face_terms([pair[0] for pair in faces], normal)
    right = face_terms([pair[1] for pair in faces], normal)
    signal = 0.5 * jnp.maximum(left[2], right[2])
    differences = []
    for k in range(FIELDS):
        flux = 0.5 * (left[1][k] + right[1][k]) - signal * (right[0][k] - left[0][k])
        differences.append(flux - shifted(flux, -1, axis))
    return differences


def beside(me, step, count):
    size = count // 2
    row = lax.rem(me, size)
    return me - row + lax.rem(row + size + step, size)


def start_kernel(me_ref, fields_ref, send_ref, own_ref, cells_ref, swapped_ref):
    count = send_ref.shape[0]
    rows, columns = fields_ref.shape[1:]
    cells = [fields_ref[k] for k in range(FIELDS)]
    for k in range(FIELDS):
        cells_ref[k] = cells[k]
    (density, *velocity, pressure), _ = primitives(cells)
    speed = jnp.maximum(jnp.abs(velocity[0]), jnp.abs(velocity[1]))
    speed = speed + jnp.sqrt(GAMMA * pressure / density)
    peak = jnp.max(speed, axis=0, keepdims=True)
    peak = jnp.maximum(peak, pltpu.roll(peak, rows, 1))
    lane = lax.broadcasted_iota(jnp.int32, (rows, columns), 1)
    ends = starts = jnp.zeros((rows, columns), jnp.float32)
    for k in range(FIELDS):
        at = k * STRIP
        turned = pltpu.roll(cells[k], at + 2 * WIDTH, 1)
        ends = jnp.where((lane >= at) & (lane < at + 2 * WIDTH), turned, ends)
        turned = pltpu.roll(cells[k], at + WIDTH, 1)
        starts = jnp.where((lane >= at + WIDTH) & (lane < at + STRIP), turned, starts)
    own = jnp.transpose(jnp.concatenate([ends, starts], axis=0))[: own_ref.shape[0]]
    own_ref[...] = own
    swapped_ref[...] = pltpu.roll(own, rows, 1)
    half = lax.broadcasted_iota(jnp.int32, (1, columns), 1) < rows

    def row_of(ref, slot):
        at = slot // WIDTH * STRIP + WIDTH + slot % WIDTH
        return ref[at : at + 1, :]

    ends, starts = [], []
    for row in range(PACKED):
        last = row == PACKED - 1
        ends.append(
            jnp.where(half, row_of(own_ref, row), peak if last else row_of(swapped_ref, PACKED + row))
        )
        starts.append(
            jnp.where(half, row_of(swapped_ref, row), peak if last else row_of(own_ref, PACKED + row))
        )
    ends, starts = jnp.concatenate(ends, axis=0), jnp.concatenate(starts, axis=0)
    for j in range(count):
        send_ref[j] = ends
    send_ref[beside(me_ref[0], -1, count)] = starts


def inner_kernel(cells_ref, change_ref):
    for row in range(0, cells_ref.shape[1], 8):
        change = flux_difference([cells_ref[k, row : row + 8, :] for k in range(FIELDS)], 1, 1)
        for k in range(FIELDS):
            change_ref[k, row : row + 8, :] = change[k]


def peak_kernel(received_ref, peak_ref):
    columns = received_ref.shape[2]
    rows = columns // 2
    half = lax.broadcasted_iota(jnp.int32, (1, columns), 1) < rows
    peak = jnp.max(received_ref[...], axis=0)[PACKED - 1 :, :]
    peak = jnp.where(half, pltpu.roll(peak, rows, 1), peak)
    peak_ref[...] = jnp.broadcast_to(peak[None], peak_ref.shape)


def edge_kernel(
    me_ref, cells_ref, inner_ref, own_ref, received_ref,
    change_ref, near_ref, far_ref, strip_ref, side_ref, turned_ref,
):
    count = received_ref.shape[0]
    rows, columns = cells_ref.shape[1:]
    me, odd = me_ref[0], me_ref[0] >= count // 2
    before, after = beside(me, -1, count), beside(me, 1, count)
    half = lax.broadcasted_iota(jnp.int32, (1, columns), 1) < rows
    side_ref[0] = received_ref[after]
    side_ref[1] = pltpu.roll(received_ref[after], rows, 1)
    side_ref[2] = received_ref[before]
    side_ref[3] = pltpu.roll(received_ref[before], rows, 1)
    for k in range(FIELDS):
        at = k * STRIP
        strip_ref[k, :STRIP, :] = own_ref[at : at + STRIP, :]
        strip_ref[k, STRIP:, :] = jnp.broadcast_to(own_ref[at + WIDTH : at + WIDTH + 1, :], (16 - STRIP, columns))
        for j in range(WIDTH):
            slot = k * WIDTH + j
            row, far = slot % PACKED, slot // PACKED
            low, high = at + j, at + 2 * WIDTH + j
            strip_ref[k, j : j + 1, :] = jnp.where(
                half, own_ref[low : low + 1, :], side_ref[2 if far else 3, row : row + 1, :]
            )
            strip_ref[k, 2 * WIDTH + j : 2 * WIDTH + j + 1, :] = jnp.where(
                half, side_ref[1 if far else 0, row : row + 1, :], own_ref[high : high + 1, :]
            )
    edge = flux_difference([strip_ref[k] for k in range(FIELDS)], 0, 1)
    turned_ref[...] = jnp.zeros_like(turned_ref)
    for k in range(FIELDS):
        turned_ref[k * WIDTH : (k + 1) * WIDTH, :] = edge[k][WIDTH : 2 * WIDTH]
    turned = jnp.transpose(turned_ref[...])
    at_end, at_start = turned[:rows], turned[rows:]
    lane = lax.broadcasted_iota(jnp.int32, (rows, columns), 1)
    for k in range(FIELDS):
        change = jnp.where(
            lane >= columns - WIDTH, pltpu.roll(at_end, columns - WIDTH - k * WIDTH, 1), inner_ref[k]
        )
        change = jnp.where(lane < WIDTH, pltpu.roll(at_start, (-k * WIDTH) % columns, 1), change)
        change_ref[k] = change
        ends = [(cells_ref[k, :WIDTH, :], cells_ref[k, rows - WIDTH :, :]), (change[:WIDTH], change[rows - WIDTH :])]
        for part, (first, last) in enumerate(ends):
            at = (part * FIELDS + k) * WIDTH
            near_ref[at : at + WIDTH, :] = jnp.where(odd, first, last)
            far_ref[at : at + WIDTH, :] = jnp.where(odd, last, first)
    near_ref[2 * FIELDS * WIDTH :, :] = jnp.zeros((2, columns), jnp.float32)
    far_ref[2 * FIELDS * WIDTH :, :] = jnp.zeros((2, columns), jnp.float32)


def sweep_kernel(count, me_ref, cells_ref, change_ref, peaks_ref, near_ref, far_ref, out_ref, half_ref):
    rows, _ = out_ref.shape[1:]
    peak = jnp.max(jnp.max(peaks_ref[...], axis=0), axis=1, keepdims=True)
    time_step = COURANT / peak
    size = FIELDS * WIDTH
    odd = me_ref[0] >= count // 2
    near = near_ref[:size, :] - time_step * near_ref[size : 2 * size, :]
    far = far_ref[:size, :] - time_step * far_ref[size : 2 * size, :]
    before, after = jnp.where(odd, near, far), jnp.where(odd, far, near)
    for k in range(FIELDS):
        half = cells_ref[k] - time_step * change_ref[k]
        half_ref[k, :rows, :] = half
        half_ref[k, rows : rows + 8, :] = half[:8]
        half_ref[k, rows : rows + WIDTH, :] = after[k * WIDTH : (k + 1) * WIDTH]
        half_ref[k, rows + 8 - WIDTH : rows + 8, :] = before[k * WIDTH : (k + 1) * WIDTH]
    cells = [half_ref[k] for k in range(FIELDS)]
    change = flux_difference(cells, 0, 2)
    for k in range(FIELDS):
        out_ref[k] = (cells[k] - time_step * change[k])[:rows]


def call(kernel, out_shape, n_smem, n_vmem, scratch=()):
    return pl.pallas_call(
        kernel,
        out_shape=out_shape,
        in_specs=[SMEM] * n_smem + [VMEM] * n_vmem,
        out_specs=jax.tree.map(lambda _: VMEM, out_shape),
        scratch_shapes=list(scratch),
        cost_estimate=pl.CostEstimate(flops=4_000_000, bytes_accessed=1_000_000, transcendentals=0),
    )


def f32(*shape):
    return jax.ShapeDtypeStruct(shape, jnp.float32)


def kept(*shape):
    return pltpu.VMEM(shape, jnp.float32)


def held(*arrays):
    return [pltpu.with_memory_space_constraint(array, pltpu.VMEM) for array in arrays]


def local(fields):
    rows, columns = fields.shape[2:]
    fields = fields.reshape(FIELDS, rows, columns)
    count_side, count_rest, count_col = lax.axis_size(SIDE), lax.axis_size(REST), lax.axis_size(COL)
    me = lax.axis_index(SIDE).astype(jnp.int32).reshape(1)
    whole = kept(FIELDS, rows, columns)
    halo = kept(32, columns)
    inside = [(i, i ^ 1) for i in range(count_col)]
    between = [(i, (i + (1 if i % 2 else -1)) % count_col) for i in range(count_col)]

    shapes = (kept(count_side, PACKED, columns), kept(48, columns), whole)
    scratch = [pltpu.VMEM((48, columns), jnp.float32)]
    send, own, cells = call(start_kernel, shapes, 1, 1, scratch)(me, fields)
    received = lax.all_to_all(send, SIDE, 0, 0, tiled=True)
    inner = call(inner_kernel, whole, 0, 1)(*held(cells))
    peak = call(peak_kernel, kept(count_rest, 1, columns), 0, 1)(*held(received))
    peaks = lax.all_to_all(peak, REST, 0, 0, tiled=True)
    scratch = [(FIELDS, 16, columns), (4, PACKED, columns), (columns, columns)]
    scratch = [pltpu.VMEM(shape, jnp.float32) for shape in scratch]
    change, near, far = call(edge_kernel, (whole, halo, halo), 1, 4, scratch)(me, *held(cells, inner, own, received))
    far = lax.ppermute(far, COL, between)
    near = lax.ppermute(near, COL, inside)
    scratch = [pltpu.VMEM((FIELDS, rows + 8, columns), jnp.float32)]
    out = call(functools.partial(sweep_kernel, count_side), f32(FIELDS, rows, columns), 1, 5, scratch)(
        me, *held(cells, change, peaks, near, far)
    )
    return out.reshape(FIELDS, 1, rows, columns)


def solution(mesh):
    split = Mesh(mesh.devices.reshape(8, 2, 8, 4, 2), (*ROW, *COL))
    placed = (P(None, None, COL, ROW),)
    return jax.shard_map(
        local, mesh=split, in_specs=placed, out_specs=P(None, None, COL, ROW), check_vma=False
    )
```

```python
import jax
import jax.numpy as jnp
from jax import lax
from jax.experimental import pallas as pl
from jax.experimental.pallas import tpu as pltpu
from jax.sharding import Mesh
from jax.sharding import PartitionSpec as P


ROW = ("row_0", "row_1")
COL = ("col_0", "col_1", "col_2")
FIRST = (ROW[0], COL[0])
SECOND = (COL[1], ROW[1], COL[2])

GAMMA = 1.4
COURANT = 0.3
WIDTH = 3
FIELDS = 5
PACKED = 8
STRIP = 9
VMEM = pl.BlockSpec(memory_space=pltpu.VMEM)
SMEM = pl.BlockSpec(memory_space=pltpu.SMEM)


def minmod(first, second):
    low = jnp.minimum(first, second)
    high = jnp.maximum(first, second)
    return jnp.maximum(low, 0.0) + jnp.minimum(high, 0.0)


def shifted(profile, step, axis):
    return pltpu.roll(profile, (-step) % profile.shape[axis], axis)


def primitives(cells):
    inverse = 1.0 / cells[0]
    velocity = [cells[k] * inverse for k in (1, 2, 3)]
    kinetic = 0.5 * (cells[1] * velocity[0] + cells[2] * velocity[1] + cells[3] * velocity[2])
    return [cells[0], *velocity, (GAMMA - 1.0) * (cells[4] - kinetic)], inverse


def rebuild(profile, axis):
    after = shifted(profile, 1, axis)
    edge = 7.0 / 12.0 * (profile + after) - 1.0 / 12.0 * (
        shifted(profile, -1, axis) + shifted(profile, 2, axis)
    )
    edge = jnp.clip(edge, jnp.minimum(profile, after), jnp.maximum(profile, after))
    rise = edge - profile
    fall = profile - shifted(edge, -1, axis)
    right = profile + minmod(rise, 2.0 * fall)
    left = profile - minmod(fall, 2.0 * rise)
    return right, shifted(left, 1, axis)


def face_terms(state, normal):
    density, pressure = state[0], state[4]
    speed = state[normal]
    momentum = [density * state[k] for k in (1, 2, 3)]
    square = state[1] * momentum[0] + state[2] * momentum[1] + state[3] * momentum[2]
    energy = pressure * (1.0 / (GAMMA - 1.0)) + 0.5 * square
    conserved = [density, *momentum, energy]
    flux = [momentum[normal - 1]]
    for k in range(3):
        term = speed * momentum[k]
        flux.append(term + pressure if k == normal - 1 else term)
    flux.append(speed * (energy + pressure))
    return conserved, flux, jnp.abs(speed) + jnp.sqrt(GAMMA * pressure / density)


def flux_difference(cells, axis, normal):
    states, _ = primitives(cells)
    faces = [rebuild(profile, axis) for profile in states]
    left = face_terms([pair[0] for pair in faces], normal)
    right = face_terms([pair[1] for pair in faces], normal)
    signal = 0.5 * jnp.maximum(left[2], right[2])
    differences = []
    for k in range(FIELDS):
        flux = 0.5 * (left[1][k] + right[1][k]) - signal * (right[0][k] - left[0][k])
        differences.append(flux - shifted(flux, -1, axis))
    return differences


def start_kernel(me_ref, fields_ref, peak_ref, near_ref, far_ref, own_ref, cells_ref, swapped_ref):
    rows, columns = fields_ref.shape[1:]
    cells = [fields_ref[k] for k in range(FIELDS)]
    for k in range(FIELDS):
        cells_ref[k] = cells[k]
    (density, *velocity, pressure), _ = primitives(cells)
    speed = jnp.maximum(jnp.abs(velocity[0]), jnp.abs(velocity[1]))
    speed = speed + jnp.sqrt(GAMMA * pressure / density)
    peak = jnp.max(speed, axis=0, keepdims=True)
    peak_ref[...] = jnp.broadcast_to(peak[None], peak_ref.shape)
    lane = lax.broadcasted_iota(jnp.int32, (rows, columns), 1)
    ends = starts = jnp.zeros((rows, columns), jnp.float32)
    for k in range(FIELDS):
        at = k * STRIP
        turned = pltpu.roll(cells[k], at + 2 * WIDTH, 1)
        ends = jnp.where((lane >= at) & (lane < at + 2 * WIDTH), turned, ends)
        turned = pltpu.roll(cells[k], at + WIDTH, 1)
        starts = jnp.where((lane >= at + WIDTH) & (lane < at + STRIP), turned, starts)
    own = jnp.transpose(jnp.concatenate([ends, starts], axis=0))[: own_ref.shape[0]]
    own_ref[...] = own
    swapped_ref[...] = pltpu.roll(own, rows, 1)
    half = lax.broadcasted_iota(jnp.int32, (1, columns), 1) < rows

    def row_of(ref, slot):
        at = slot // WIDTH * STRIP + WIDTH + slot % WIDTH
        return ref[at : at + 1, :]

    ends, starts = [], []
    for row in range(PACKED):
        high = min(PACKED + row, FIELDS * WIDTH - 1)
        ends.append(jnp.where(half, row_of(own_ref, row), row_of(swapped_ref, high)))
        starts.append(jnp.where(half, row_of(swapped_ref, row), row_of(own_ref, high)))
    ends, starts = jnp.concatenate(ends, axis=0), jnp.concatenate(starts, axis=0)
    odd = me_ref[0] >= 2
    near_ref[...] = jnp.where(odd, starts, ends)
    far_ref[...] = jnp.where(odd, ends, starts)


def inner_kernel(cells_ref, change_ref):
    for row in range(0, cells_ref.shape[1], 8):
        change = flux_difference([cells_ref[k, row : row + 8, :] for k in range(FIELDS)], 1, 1)
        for k in range(FIELDS):
            change_ref[k, row : row + 8, :] = change[k]


def peak_kernel(received_ref, peak_ref):
    peak_ref[...] = jnp.broadcast_to(jnp.max(received_ref[...], axis=0)[None], peak_ref.shape)


def edge_kernel(
    me_ref, cells_ref, inner_ref, own_ref, near_side_ref, far_side_ref,
    change_ref, near_ref, far_ref, strip_ref, side_ref, turned_ref,
):
    rows, columns = cells_ref.shape[1:]
    odd_row, odd = me_ref[0] >= 2, lax.rem(me_ref[0], 2) == 1
    half = lax.broadcasted_iota(jnp.int32, (1, columns), 1) < rows
    after = jnp.where(odd_row, far_side_ref[...], near_side_ref[...])
    before = jnp.where(odd_row, near_side_ref[...], far_side_ref[...])
    side_ref[0] = after
    side_ref[1] = pltpu.roll(after, rows, 1)
    side_ref[2] = before
    side_ref[3] = pltpu.roll(before, rows, 1)
    for k in range(FIELDS):
        at = k * STRIP
        strip_ref[k, :STRIP, :] = own_ref[at : at + STRIP, :]
        strip_ref[k, STRIP:, :] = jnp.broadcast_to(own_ref[at + WIDTH : at + WIDTH + 1, :], (16 - STRIP, columns))
        for j in range(WIDTH):
            slot = k * WIDTH + j
            row, far = slot % PACKED, slot // PACKED
            low, high = at + j, at + 2 * WIDTH + j
            strip_ref[k, j : j + 1, :] = jnp.where(
                half, own_ref[low : low + 1, :], side_ref[2 if far else 3, row : row + 1, :]
            )
            strip_ref[k, 2 * WIDTH + j : 2 * WIDTH + j + 1, :] = jnp.where(
                half, side_ref[1 if far else 0, row : row + 1, :], own_ref[high : high + 1, :]
            )
    edge = flux_difference([strip_ref[k] for k in range(FIELDS)], 0, 1)
    turned_ref[...] = jnp.zeros_like(turned_ref)
    for k in range(FIELDS):
        turned_ref[k * WIDTH : (k + 1) * WIDTH, :] = edge[k][WIDTH : 2 * WIDTH]
    turned = jnp.transpose(turned_ref[...])
    at_end, at_start = turned[:rows], turned[rows:]
    lane = lax.broadcasted_iota(jnp.int32, (rows, columns), 1)
    for k in range(FIELDS):
        change = jnp.where(
            lane >= columns - WIDTH, pltpu.roll(at_end, columns - WIDTH - k * WIDTH, 1), inner_ref[k]
        )
        change = jnp.where(lane < WIDTH, pltpu.roll(at_start, (-k * WIDTH) % columns, 1), change)
        change_ref[k] = change
        ends = [(cells_ref[k, :WIDTH, :], cells_ref[k, rows - WIDTH :, :]), (change[:WIDTH], change[rows - WIDTH :])]
        for part, (first, last) in enumerate(ends):
            at = (part * FIELDS + k) * WIDTH
            near_ref[at : at + WIDTH, :] = jnp.where(odd, first, last)
            far_ref[at : at + WIDTH, :] = jnp.where(odd, last, first)
    near_ref[2 * FIELDS * WIDTH :, :] = jnp.zeros((2, columns), jnp.float32)
    far_ref[2 * FIELDS * WIDTH :, :] = jnp.zeros((2, columns), jnp.float32)


def sweep_kernel(me_ref, cells_ref, change_ref, peaks_ref, near_ref, far_ref, out_ref, half_ref):
    rows, _ = out_ref.shape[1:]
    peak = jnp.max(jnp.max(peaks_ref[...], axis=0), axis=1, keepdims=True)
    time_step = COURANT / peak
    size = FIELDS * WIDTH
    odd = lax.rem(me_ref[0], 2) == 1
    near = near_ref[:size, :] - time_step * near_ref[size : 2 * size, :]
    far = far_ref[:size, :] - time_step * far_ref[size : 2 * size, :]
    before, after = jnp.where(odd, near, far), jnp.where(odd, far, near)
    for k in range(FIELDS):
        half = cells_ref[k] - time_step * change_ref[k]
        half_ref[k, :rows, :] = half
        half_ref[k, rows : rows + 8, :] = half[:8]
        half_ref[k, rows : rows + WIDTH, :] = after[k * WIDTH : (k + 1) * WIDTH]
        half_ref[k, rows + 8 - WIDTH : rows + 8, :] = before[k * WIDTH : (k + 1) * WIDTH]
    cells = [half_ref[k] for k in range(FIELDS)]
    change = flux_difference(cells, 0, 2)
    for k in range(FIELDS):
        out_ref[k] = (cells[k] - time_step * change[k])[:rows]


def call(kernel, out_shape, n_smem, n_vmem, scratch=()):
    return pl.pallas_call(
        kernel,
        out_shape=out_shape,
        in_specs=[SMEM] * n_smem + [VMEM] * n_vmem,
        out_specs=jax.tree.map(lambda _: VMEM, out_shape),
        scratch_shapes=list(scratch),
        cost_estimate=pl.CostEstimate(flops=4_000_000, bytes_accessed=1_000_000, transcendentals=0),
    )


def f32(*shape):
    return jax.ShapeDtypeStruct(shape, jnp.float32)


def kept(*shape):
    return pltpu.VMEM(shape, jnp.float32)


def held(*arrays):
    return [pltpu.with_memory_space_constraint(array, pltpu.VMEM) for array in arrays]


def local(fields):
    rows, columns = fields.shape[2:]
    fields = fields.reshape(FIELDS, rows, columns)
    count_first, count_second = lax.axis_size(FIRST), lax.axis_size(SECOND)
    me = (lax.axis_index(ROW[1]) * 2 + lax.axis_index(COL[2])).astype(jnp.int32).reshape(1)
    whole = kept(FIELDS, rows, columns)
    halo, side = kept(32, columns), kept(PACKED, columns)

    def pairings(axes):
        count = lax.axis_size(axes)
        near = [(i, i ^ 1) for i in range(count)]
        return near, [(i, (i + (1 if i % 2 else -1)) % count) for i in range(count)]

    inside_row, between_row = pairings(ROW)
    inside, between = pairings(COL)
    shapes = (kept(count_first, 1, columns), side, side, kept(48, columns), whole)
    scratch = [pltpu.VMEM((48, columns), jnp.float32)]
    peak, near_side, far_side, own, cells = call(start_kernel, shapes, 1, 1, scratch)(me, fields)
    received = lax.all_to_all(peak, FIRST, 0, 0, tiled=True)
    far_side = lax.ppermute(far_side, ROW, between_row)
    near_side = lax.ppermute(near_side, ROW, inside_row)
    inner = call(inner_kernel, whole, 0, 1)(*held(cells))
    peak = call(peak_kernel, kept(count_second, 1, columns), 0, 1)(*held(received))
    peaks = lax.all_to_all(peak, SECOND, 0, 0, tiled=True)
    scratch = [(FIELDS, 16, columns), (4, PACKED, columns), (columns, columns)]
    scratch = [pltpu.VMEM(shape, jnp.float32) for shape in scratch]
    change, near, far = call(edge_kernel, (whole, halo, halo), 1, 5, scratch)(
        me, *held(cells, inner, own, near_side, far_side)
    )
    far = lax.ppermute(far, COL, between)
    near = lax.ppermute(near, COL, inside)
    scratch = [pltpu.VMEM((FIELDS, rows + 8, columns), jnp.float32)]
    out = call(sweep_kernel, f32(FIELDS, rows, columns), 1, 5, scratch)(
        me, *held(cells, change, peaks, near, far)
    )
    return out.reshape(FIELDS, 1, rows, columns)


def solution(mesh):
    split = Mesh(mesh.devices.reshape(8, 2, 8, 4, 2), (*ROW, *COL))
    placed = (P(None, None, COL, ROW),)
    return jax.shard_map(
        local, mesh=split, in_specs=placed, out_specs=P(None, None, COL, ROW), check_vma=False
    )
```
